512 devices in a mesh: expert: 64 (over y, z), dp: 8 (over x, core).
Axes of the slice: x: 4, y: 8, z: 8, core: 2. Of those that a mesh axis runs over, the one named last changes fastest.
Arguments:
- tokens: bfloat16 [8192, 3584], P(('dp', 'expert')), parts along dimension 0, may hold values from -6 to 6
- expert_ids: int32 [8192, 2], P(('dp', 'expert')), parts along dimension 0, may hold values from 0 to 5, as said below
- gate_weights: float32 [8192, 2], P(('dp', 'expert')), parts along dimension 0, may hold values from 0.1 to 1
- replica_pick: int32 [8192, 2], P(('dp', 'expert')), parts along dimension 0, may hold values from 0 to 1
- placement: int32 [8], replicated, may hold values from 0 to 5, as said below
- w_in: bfloat16 [2, 3584, 8192], P(None, None, 'expert')
- w_out: bfloat16 [8192, 3584], P('expert')
Outputs:
- moe_out: bfloat16 [8192, 3584], P(('dp', 'expert')), parts along dimension 0
The draws below stay inside these ranges and needn't reach their ends.
There are 8 independent parts, one for each index of `dp`. The reference program is written for one: setup_inputs(seed, part) draws one part's arguments, and reference() takes and returns one part's arrays. A program takes and returns all parts, laid end to end along the dimension named above; an argument that names none is the same for every part. Nothing has to cross between parts.
Inputs may be any that keep to these rules, and one draw needn't show every extreme that they name: `expert_ids`: each row names 2 different experts. `placement`: every expert is named once or twice, 2 of them twice, at any positions.
All inputs are finite; a program needn't handle non-finite values.
Results may differ from the reference program's by a relative error of at most 0.012.
Values may be sent and summed in bfloat16 or wider, within the bound.
A program may use at most 64 MiB of HBM per device.

```python
import jax
import jax.numpy as jnp
from jax import lax

D = 3584
F = 1024
TOP = 2
T_DEV = 16
SPLIT = 8
F_DEV = 128
PHYS = 8
REPL = 2
LOG = 6
CAP = 4
TOKENS = 1024
N_EXPERT = 64


def layout(key):
    base_key = jax.random.fold_in(key, 11)
    every_expert = jnp.arange(LOG, dtype=jnp.int32)
    hot_experts = jax.random.permutation(jax.random.fold_in(base_key, 2), LOG)[:REPL].astype(jnp.int32)
    listed = jnp.concatenate([every_expert, hot_experts]).astype(jnp.int32)
    order = jax.random.permutation(jax.random.fold_in(base_key, 3), PHYS).astype(jnp.int32)
    return jnp.take(listed, order).astype(jnp.int32)


def draw_placement(key, part):
    return layout(key)


def draw_expert_ids(key, part):
    scores = jax.random.randint(jax.random.fold_in(key, 41), (TOKENS, LOG), 0, 1000, dtype=jnp.int32)
    expert_index = jnp.arange(LOG, dtype=jnp.int32)
    ranking = jax.random.permutation(jax.random.fold_in(key, 43), LOG).astype(jnp.int32)
    favour = jnp.where(ranking < REPL, 600, 0).astype(jnp.int32)
    distinct = (scores + favour[None, :]) * LOG + expert_index[None, :]
    return lax.top_k(distinct, TOP)[1].astype(jnp.int32)


def weight_base(key, shape):
    return jax.random.normal(key, shape, jnp.float32)


def draw_w_in(key, part):
    places = layout(key)
    base = weight_base(jax.random.fold_in(key, 21), (2, D, LOG, F)) * D ** (-0.5)
    taken = jnp.take(base, places, axis=2)
    return taken.reshape(2, D, PHYS * F).astype(jnp.bfloat16)


def draw_w_out(key, part):
    places = layout(key)
    base = weight_base(jax.random.fold_in(key, 31), (LOG, F, D)) * F ** (-0.5)
    taken = jnp.take(base, places, axis=0)
    return taken.reshape(PHYS * F, D).astype(jnp.bfloat16)


def place_ends(array, stream_key, least, largest):
    dims = array.shape
    place = [jax.random.randint(jax.random.fold_in(stream_key, axis), (), 0, dims[axis]) for axis in range(len(dims))]
    array = array.at[tuple(place)].set(least)
    longest = dims.index(max(dims))
    place[longest] = (place[longest] + 1) % dims[longest]
    return array.at[tuple(place)].set(largest)


def shard_levels(own_key, extent, split, low, high):
    loudness, own = 1.0, jax.random.fold_in(own_key, 6)
    for position, parts in split:
        draws = jnp.exp(jax.random.uniform(jax.random.fold_in(own, position), (parts,), jnp.float32, low / len(split), high / len(split)))
        loudness = loudness * jnp.repeat(draws, extent[position] // parts).reshape([-1 if axis == position else 1 for axis in range(len(extent))])
    return loudness


def gaussian(rng, dims, scale, limit, shards=(), kind=jnp.bfloat16):
    array = scale * jax.random.normal(rng, dims, jnp.float32)
    if shards:
        array = array * shard_levels(rng, dims, shards, -0.22, 0.18)
    return jnp.clip(array, -limit, limit).astype(kind)


def setup_inputs(seed: int = 0, part: int = 0) -> dict:
    seeds = jax.random.split(jax.random.key(seed), 8)
    own_keys = jax.random.split(jax.random.fold_in(seeds[7], part), 8)
    tokens = gaussian(own_keys[0], (TOKENS, D), 1.0, 6.0, ((0, 64),))
    expert_ids = draw_expert_ids(jax.random.fold_in(jax.random.fold_in(seeds[7], part), 71), part)
    gate_weights = jnp.clip(0.1 + 0.9 * jax.random.uniform(own_keys[2], (TOKENS, TOP), jnp.float32) ** shard_levels(own_keys[2], (TOKENS, TOP), ((0, 64),), -0.2, 0.2), 0.1, 1.0)
    replica_pick = place_ends(jax.random.randint(own_keys[3], (TOKENS, TOP), 0, 2), jax.random.fold_in(own_keys[3], 1), 0, 1).astype(jnp.int32)
    placement = draw_placement(jax.random.fold_in(seeds[7], 71), part)
    w_in = draw_w_in(jax.random.fold_in(seeds[7], 71), part)
    w_out = draw_w_out(jax.random.fold_in(seeds[7], 71), part)
    return dict(tokens=tokens, expert_ids=expert_ids, gate_weights=gate_weights, replica_pick=replica_pick, placement=placement, w_in=w_in, w_out=w_out)


def route_block(expert_ids, replica_pick, gate_weights, placement, slot_count, capacity):
    tok_count, top_count = expert_ids.shape
    copy_index = jnp.arange(slot_count, dtype=jnp.int32)
    same_expert = placement[:, None] == placement[None, :]
    before = jnp.sum((same_expert & (copy_index[:, None] < copy_index[None, :])).astype(jnp.int32), axis=0)
    matches = placement[None, None, :] == expert_ids[:, :, None]
    copies = jnp.sum(matches.astype(jnp.int32), axis=-1)
    wanted = replica_pick % copies
    chosen = (matches & (before[None, None, :] == wanted[:, :, None])).astype(jnp.int32)
    flat_hot = chosen.reshape(tok_count * top_count, slot_count)
    earlier = jnp.cumsum(flat_hot, axis=0) - flat_hot
    slot_rank = jnp.sum(earlier * flat_hot, axis=-1).reshape(tok_count, top_count)
    slot_index = jnp.arange(capacity, dtype=jnp.int32)
    in_slot = chosen[:, :, :, None] * (slot_rank[:, :, None, None] == slot_index[None, None, None, :]).astype(jnp.int32)
    in_slot = in_slot.astype(jnp.float32)
    pick_rows = jnp.sum(in_slot, axis=1).reshape(tok_count, slot_count * capacity).T
    combine_rows = jnp.sum(in_slot * gate_weights[:, :, None, None], axis=1).reshape(tok_count, slot_count * capacity)
    return pick_rows, combine_rows


def expert_copy(args):
    received, gate_w, up_w, down_w = args
    gate = jnp.dot(received, gate_w, preferred_element_type=jnp.float32)
    upper = jnp.dot(received, up_w, preferred_element_type=jnp.float32)
    hidden = (jax.nn.silu(gate) * upper).astype(jnp.bfloat16)
    hidden_blocks = hidden.reshape(received.shape[0], SPLIT, F_DEV).astype(jnp.float32)
    down_blocks = down_w.reshape(SPLIT, F_DEV, D).astype(jnp.float32)
    partial_value = jnp.einsum("rjf,jfd->jrd", hidden_blocks, down_blocks).astype(jnp.bfloat16)
    return jnp.sum(partial_value.astype(jnp.float32), axis=0)


def reference(tokens, expert_ids, gate_weights, replica_pick, placement, w_in, w_out):
    tok_blocks = tokens.reshape(N_EXPERT, T_DEV, D)
    id_blocks = expert_ids.reshape(N_EXPERT, T_DEV, TOP)
    pick_blocks = replica_pick.reshape(N_EXPERT, T_DEV, TOP)
    gate_blocks = gate_weights.reshape(N_EXPERT, T_DEV, TOP)
    pick_rows, combine_rows = jax.vmap(lambda a, b, c: route_block(a, b, c, placement, PHYS, CAP))(id_blocks, pick_blocks, gate_blocks)
    slot_rows = jnp.einsum("spt,std->spd", pick_rows, tok_blocks.astype(jnp.float32)).astype(jnp.bfloat16)
    slot_rows = slot_rows.reshape(N_EXPERT, PHYS, CAP, D).transpose(1, 0, 2, 3).reshape(PHYS, N_EXPERT * CAP, D)
    gate_all = w_in[0].reshape(D, PHYS, F).transpose(1, 0, 2)
    up_all = w_in[1].reshape(D, PHYS, F).transpose(1, 0, 2)
    down_all = w_out.reshape(PHYS, F, D)
    expert_out = lax.map(expert_copy, (slot_rows, gate_all, up_all, down_all))
    expert_out = expert_out.reshape(PHYS, N_EXPERT, CAP, D).transpose(1, 0, 2, 3).reshape(N_EXPERT, PHYS * CAP, D)
    moe_out = jnp.einsum("stk,skd->std", combine_rows, expert_out, precision=lax.Precision.HIGHEST)
    return moe_out.reshape(TOKENS, D).astype(jnp.bfloat16)
```

```python
import functools

import jax
import jax.numpy as jnp
from jax import lax
from jax.experimental import pallas as pl
from jax.experimental.pallas import tpu as pltpu
from jax.sharding import PartitionSpec as P

N = 8
OFFS = (0, 1, -1, 2, -2, 3, -3, 4)
FOLD = 4
CAP = 4
ROWS = FOLD * CAP
MESH = pl.DeviceIdType.MESH
F32 = jnp.float32
BF16 = jnp.bfloat16
FAR = ((0, 1), (2, 3))


def iota(shape, axis):
    return lax.broadcasted_iota(jnp.int32, shape, axis)


def routing(y, ids_ref, gw_ref, pick_ref, place_ref, pad):
    tok = ids_ref.shape[1]
    pad[...] = jnp.zeros_like(pad)
    pad[0:2, 0:tok] = ids_ref[...].astype(F32)
    pad[2:4, 0:tok] = pick_ref[...].astype(F32)
    pad[4:6, 0:tok] = gw_ref[...]
    pad[8:9, 0:N] = place_ref[...].astype(F32)
    wide = pad[0:8, :]
    wide = (
        wide
        + pltpu.roll(wide, tok, 1)
        + pltpu.roll(wide, 2 * tok, 1)
        + pltpu.roll(wide, 3 * tok, 1)
    )
    place_row = jnp.broadcast_to(pad[8:9, :], (N, 128))
    sub, lane = iota((N, 128), 0), iota((N, 128), 1)
    place_col = jnp.sum(jnp.where(sub == lane, place_row, 0.0), axis=1, keepdims=True)
    before = jnp.sum(
        jnp.where((place_row == place_col) & (lane < sub), 1.0, 0.0), axis=1, keepdims=True
    )
    subf = sub.astype(F32)
    row, col = iota((128, 128), 0), iota((128, 128), 1)
    j = row // ROWS
    offs = jnp.where(j % 2 == 1, (j + 1) // 2, -(j // 2))
    copy_of_row = ((y - offs + N) % N).astype(F32)
    chosen = []
    for k in range(2):
        match = place_col == wide[k : k + 1, :]
        copies = jnp.sum(jnp.where(match, 1.0, 0.0), axis=0, keepdims=True)
        wanted = jnp.where(copies > 1.5, wide[2 + k : 3 + k, :], 0.0)
        phys = jnp.sum(
            jnp.where(match & (before == wanted), subf, 0.0), axis=0, keepdims=True
        )
        chosen.append(jnp.where(copy_of_row == phys, 1.0, 0.0))
    earlier = jnp.where((row // tok == col // tok) & (row < col), 1.0, 0.0).astype(BF16)
    rank = jnp.dot((chosen[0] + chosen[1]).astype(BF16), earlier, preferred_element_type=F32)
    own = col // tok == (row // CAP) % FOLD
    slot = (row % CAP).astype(F32)
    in0 = jnp.where(own & (rank == slot), chosen[0], 0.0)
    in1 = jnp.where(own & (rank + chosen[0] == slot), chosen[1], 0.0)
    pick = (in0 + in1).astype(BF16)
    combine = in0 * wide[4:5, :] + in1 * wide[5:6, :]
    return pick, combine.T


def kernel(
    ids_ref, gw_ref, pick_ref, place_ref, tok_ref, win_ref, wout_ref, out_ref,
    pad, w1, w2, comb, ybuf, xbuf, xrows, part, sbuf, rbuf, obuf, cbuf,
    wsem, yds, ydr, ags, agr, rss, rsr, yrs, yrr,
):
    wide = tok_ref.shape[1] // FOLD
    units = w2.shape[0]
    e = lax.axis_index("expert")
    y, z = e // N, e % N
    right = y * N + (z + 1) % N
    left = y * N + (z + N - 1) % N
    side = (right, left)

    loads = [
        pltpu.make_async_copy(win_ref.at[0], w1.at[:, 0:units], wsem.at[0]),
        pltpu.make_async_copy(win_ref.at[1], w1.at[:, units : 2 * units], wsem.at[1]),
        pltpu.make_async_copy(wout_ref, w2, wsem.at[2]),
    ]
    for load in loads:
        load.start()

    barrier = pltpu.get_barrier_semaphore()
    peers = [(y + d) % N * N + z for d in range(1, N)] + [right, left]
    for peer in peers:
        pl.semaphore_signal(barrier, inc=1, device_id={"expert": peer}, device_id_type=MESH)

    pick, combine = routing(y, ids_ref, gw_ref, pick_ref, place_ref, pad)
    tok_fold = jnp.concatenate(
        [tok_ref[:, q * wide : (q + 1) * wide] for q in range(FOLD)], axis=0
    )
    messages = jnp.dot(
        pick[:, : tok_fold.shape[0]], tok_fold, preferred_element_type=F32
    ).astype(BF16)
    ybuf[...] = messages
    xbuf[0, 0, 0:ROWS, :] = messages[0:ROWS]
    half_rows = combine[: tok_fold.shape[0]]
    high = half_rows.astype(BF16)
    comb[...] = jnp.concatenate([high, (half_rows - high.astype(F32)).astype(BF16)], axis=0)

    pl.semaphore_wait(barrier, len(peers))

    def remote(src, dst, send, recv, target):
        return pltpu.make_async_remote_copy(
            src_ref=src, dst_ref=dst, send_sem=send, recv_sem=recv,
            device_id={"expert": target}, device_id_type=MESH,
        )

    def msg(i):
        return slice(i * ROWS, (i + 1) * ROWS)

    sends = []

    y_in = {}
    for j in range(1, N):
        copy = remote(
            ybuf.at[msg(j)], xbuf.at[j // 4, 0, msg(j % 4)], yds.at[j], ydr.at[j],
            (y - OFFS[j] + N) % N * N + z,
        )
        copy.start()
        sends.append(copy)
        y_in[j] = copy

    gather = {}

    def gather_step(h, s):
        for i in range(4):
            for d in range(2):
                if s == 0:
                    if d == 0 and h * 4 + i > 0:
                        y_in[h * 4 + i].wait_recv()
                else:
                    gather[h, d, s - 1, i].wait_recv()
                if s == 3 and i not in FAR[d]:
                    continue
                src = (N - s) % N if d == 0 else s
                dst = N - 1 - s if d == 0 else s + 1
                copy = remote(
                    xbuf.at[h, src, msg(i)], xbuf.at[h, dst, msg(i)],
                    ags.at[h, d, s, i], agr.at[h, d, s, i], side[d],
                )
                copy.start()
                sends.append(copy)
                gather[h, d, s, i] = copy

    a, b = iota((4 * ROWS, 4 * ROWS), 0), iota((4 * ROWS, 4 * ROWS), 1)
    swap = jnp.where(
        (a // 16 == (b // 4) % 4) & ((a // 4) % 4 == b // 16) & (a % 4 == b % 4), 1.0, 0.0
    ).astype(BF16)

    def unfold(h, slot):
        rows = jnp.dot(swap, xbuf[h, slot], preferred_element_type=F32).astype(BF16)
        for q in range(FOLD):
            xrows[h, slot * ROWS : (slot + 1) * ROWS, q * wide : (q + 1) * wide] = rows[msg(q)]

    def hidden_of(h):
        gate_up = jnp.dot(xrows[h], w1[...], preferred_element_type=F32)
        gate = gate_up[:, :units]
        return (gate / (1.0 + jnp.exp(-gate)) * gate_up[:, units:]).astype(BF16)

    def down(h, hidden):
        for q in range(FOLD):
            part[h, q] = jnp.dot(
                hidden, w2[:, q * wide : (q + 1) * wide], preferred_element_type=F32
            )

    reduce = {}

    def reduce_step(h, s):
        for fresh in (True, False):
            for q in range(FOLD):
                for d in range(2):
                    known = s > 0 and (s > 1 or q in FAR[d])
                    if known == fresh or (s == 0 and q not in FAR[d]):
                        continue
                    slot = 4 - s if d == 0 else 4 + s
                    value = part[h, q, slot * ROWS : (slot + 1) * ROWS, :]
                    if known:
                        reduce[h, d, s - 1, q].wait_recv()
                        value = value + rbuf[h, d, s - 1, q].astype(F32)
                    sbuf[h, d, s, q] = value.astype(BF16)
                    copy = remote(
                        sbuf.at[h, d, s, q], rbuf.at[h, d, s, q],
                        rss.at[h, d, s, q], rsr.at[h, d, s, q], side[d],
                    )
                    copy.start()
                    sends.append(copy)
                    reduce[h, d, s, q] = copy

    back = {}

    def finish(h):
        sums = []
        for q in range(FOLD):
            value = part[h, q, 0:ROWS, :]
            for d in range(2):
                reduce[h, d, 3, q].wait_recv()
                value = value + rbuf[h, d, 3, q].astype(F32)
            sums.append(value.astype(BF16))
        folded = jnp.dot(
            swap, jnp.concatenate(sums, axis=0), preferred_element_type=F32
        ).astype(BF16)
        obuf[h] = folded
        for i in reversed(range(4)):
            j = h * 4 + i
            if j == 0:
                cbuf[0:ROWS, :] = folded[0:ROWS]
                continue
            copy = remote(
                obuf.at[h, msg(i)], cbuf.at[msg(j)], yrs.at[j], yrr.at[j],
                (y + OFFS[j] + N) % N * N + z,
            )
            copy.start()
            sends.append(copy)
            back[j] = copy

    def gather_last(h):
        for d in range(2):
            for i in FAR[d]:
                gather[h, d, 3, i].wait_recv()

    for s in range(4):
        gather_step(0, s)
        unfold(0, (N - s) % N)
        if s > 0:
            unfold(0, s)
    gather_step(1, 0)
    unfold(1, 0)
    gather_last(0)
    unfold(0, 4)
    loads[0].wait()
    loads[1].wait()
    gather_step(1, 1)
    hidden0 = hidden_of(0)
    unfold(1, 7)
    unfold(1, 1)
    gather_step(1, 2)
    loads[2].wait()
    down(0, hidden0)
    unfold(1, 6)
    unfold(1, 2)
    gather_step(1, 3)
    reduce_step(0, 0)
    unfold(1, 5)
    unfold(1, 3)
    reduce_step(0, 1)
    gather_last(1)
    unfold(1, 4)
    hidden1 = hidden_of(1)
    reduce_step(0, 2)
    down(1, hidden1)
    reduce_step(0, 3)
    reduce_step(1, 0)
    reduce_step(1, 1)
    finish(0)
    reduce_step(1, 2)
    reduce_step(1, 3)
    finish(1)
    for j in range(1, N):
        back[j].wait_recv()
    both = jnp.dot(comb[...], cbuf[...], preferred_element_type=F32)
    half = both.shape[0] // 2
    result = both[:half] + both[half:]
    tok = out_ref.shape[0]
    for q in range(FOLD):
        out_ref[:, q * wide : (q + 1) * wide] = result[q * tok : (q + 1) * tok].astype(BF16)
    for copy in sends:
        copy.wait_send()


def body(tokens, expert_ids, gate_weights, replica_pick, placement, w_in, w_out):
    tok, width = tokens.shape
    units = w_out.shape[0]
    wide = width // FOLD
    vmem = pl.BlockSpec(memory_space=pltpu.VMEM)
    anywhere = pl.BlockSpec(memory_space=pl.ANY)
    dma = pltpu.SemaphoreType.DMA
    return pl.pallas_call(
        kernel,
        out_shape=jax.ShapeDtypeStruct((tok, width), BF16),
        in_specs=[vmem] * 5 + [anywhere] * 2,
        out_specs=vmem,
        scratch_shapes=[
            pltpu.VMEM((16, 128), F32),
            pltpu.VMEM((width, 2 * units), BF16),
            pltpu.VMEM((units, width), BF16),
            pltpu.VMEM((2 * FOLD * tok, 128), BF16),
            pltpu.VMEM((N * ROWS, wide), BF16),
            pltpu.VMEM((2, N, 4 * ROWS, wide), BF16),
            pltpu.VMEM((2, N * ROWS, width), BF16),
            pltpu.VMEM((2, FOLD, N * ROWS, wide), F32),
            pltpu.VMEM((2, 2, 4, FOLD, ROWS, wide), BF16),
            pltpu.VMEM((2, 2, 4, FOLD, ROWS, wide), BF16),
            pltpu.VMEM((2, 4 * ROWS, wide), BF16),
            pltpu.VMEM((N * ROWS, wide), BF16),
            dma((3,)),
            dma((N,)),
            dma((N,)),
            dma((2, 2, 4, 4)),
            dma((2, 2, 4, 4)),
            dma((2, 2, 4, 4)),
            dma((2, 2, 4, 4)),
            dma((N,)),
            dma((N,)),
        ],
        compiler_params=pltpu.CompilerParams(collective_id=0, has_side_effects=True),
    )(
        expert_ids.T, gate_weights.T, replica_pick.T, placement.reshape(1, -1),
        tokens, w_in, w_out,
    )


def solution(mesh):
    in_specs = (
        P(("dp", "expert"), None),
        P(("dp", "expert"), None),
        P(("dp", "expert"), None),
        P(("dp", "expert"), None),
        P(),
        P(None, None, "expert"),
        P("expert", None),
    )
    out_specs = P(("dp", "expert"), None)
    return jax.shard_map(body, mesh=mesh, in_specs=in_specs, out_specs=out_specs, check_vma=False)
```

```python
import functools

import jax
import jax.numpy as jnp
from jax import lax
from jax.experimental import pallas as pl
from jax.experimental.pallas import tpu as pltpu
from jax.sharding import PartitionSpec as P

N = 8
OFFS = (0, 1, -1, 2, -2, 3, -3, 4)
FOLD = 4
CAP = 4
ROWS = FOLD * CAP
MESH = pl.DeviceIdType.MESH
F32 = jnp.float32
BF16 = jnp.bfloat16
FAR = ((0, 1), (2, 3))
Y_TIME = (0.0, 2.5, 2.5, 3.3, 3.4, 4.2, 4.2, 5.0)


def iota(shape, axis):
    return lax.broadcasted_iota(jnp.int32, shape, axis)


def routing(y, ids_ref, gw_ref, pick_ref, place_ref, pad):
    tok = ids_ref.shape[1]
    pad[...] = jnp.zeros_like(pad)
    pad[0:2, 0:tok] = ids_ref[...].astype(F32)
    pad[2:4, 0:tok] = pick_ref[...].astype(F32)
    pad[4:6, 0:tok] = gw_ref[...]
    pad[8:9, 0:N] = place_ref[...].astype(F32)
    wide = pad[0:8, :]
    wide = (
        wide
        + pltpu.roll(wide, tok, 1)
        + pltpu.roll(wide, 2 * tok, 1)
        + pltpu.roll(wide, 3 * tok, 1)
    )
    place_row = jnp.broadcast_to(pad[8:9, :], (N, 128))
    sub, lane = iota((N, 128), 0), iota((N, 128), 1)
    place_col = jnp.sum(jnp.where(sub == lane, place_row, 0.0), axis=1, keepdims=True)
    before = jnp.sum(
        jnp.where((place_row == place_col) & (lane < sub), 1.0, 0.0), axis=1, keepdims=True
    )
    subf = sub.astype(F32)
    row, col = iota((128, 128), 0), iota((128, 128), 1)
    j = row // ROWS
    offs = jnp.where(j % 2 == 1, (j + 1) // 2, -(j // 2))
    copy_of_row = ((y - offs + N) % N).astype(F32)
    chosen = []
    for k in range(2):
        match = place_col == wide[k : k + 1, :]
        copies = jnp.sum(jnp.where(match, 1.0, 0.0), axis=0, keepdims=True)
        wanted = jnp.where(copies > 1.5, wide[2 + k : 3 + k, :], 0.0)
        phys = jnp.sum(
            jnp.where(match & (before == wanted), subf, 0.0), axis=0, keepdims=True
        )
        chosen.append(jnp.where(copy_of_row == phys, 1.0, 0.0))
    earlier = jnp.where((row // tok == col // tok) & (row < col), 1.0, 0.0).astype(BF16)
    rank = jnp.dot((chosen[0] + chosen[1]).astype(BF16), earlier, preferred_element_type=F32)
    own = col // tok == (row // CAP) % FOLD
    slot = (row % CAP).astype(F32)
    in0 = jnp.where(own & (rank == slot), chosen[0], 0.0)
    in1 = jnp.where(own & (rank + chosen[0] == slot), chosen[1], 0.0)
    pick = (in0 + in1).astype(BF16)
    combine = in0 * wide[4:5, :] + in1 * wide[5:6, :]
    return pick, combine.T


def kernel(
    ids_ref, gw_ref, pick_ref, place_ref, tok_ref, win_ref, wout_ref, out_ref,
    pad, w1, w2, comb, ybuf, xbuf, xrows, part, sbuf, rbuf, obuf, cbuf,
    wsem, sent, ydr, agr, agl, rsr, rsl, yrr,
):
    wide = tok_ref.shape[1] // FOLD
    units = w2.shape[0]
    e = lax.axis_index("expert")
    y, z = e // N, e % N
    right = y * N + (z + 1) % N
    left = y * N + (z + N - 1) % N
    side = (right, left)

    loads = [
        pltpu.make_async_copy(win_ref.at[0], w1.at[:, 0:units], wsem.at[0]),
        pltpu.make_async_copy(win_ref.at[1], w1.at[:, units : 2 * units], wsem.at[1]),
        pltpu.make_async_copy(wout_ref, w2, wsem.at[2]),
    ]
    for load in loads:
        load.start()

    barrier = pltpu.get_barrier_semaphore()
    peers = [(y + d) % N * N + z for d in range(1, N)] + [right, left]
    for peer in peers:
        pl.semaphore_signal(barrier, inc=1, device_id={"expert": peer}, device_id_type=MESH)

    pick, combine = routing(y, ids_ref, gw_ref, pick_ref, place_ref, pad)
    tok_fold = jnp.concatenate(
        [tok_ref[:, q * wide : (q + 1) * wide] for q in range(FOLD)], axis=0
    )
    messages = jnp.dot(
        pick[:, : tok_fold.shape[0]], tok_fold, preferred_element_type=F32
    ).astype(BF16)
    ybuf[...] = messages
    xbuf[0, 0, 0:ROWS, :] = messages[0:ROWS]
    half_rows = combine[: tok_fold.shape[0]]
    high = half_rows.astype(BF16)
    comb[...] = jnp.concatenate([high, (half_rows - high.astype(F32)).astype(BF16)], axis=0)

    pl.semaphore_wait(barrier, len(peers))

    def remote(src, dst, send, recv, target):
        return pltpu.make_async_remote_copy(
            src_ref=src, dst_ref=dst, send_sem=send, recv_sem=recv,
            device_id={"expert": target}, device_id_type=MESH,
        )

    def msg(i):
        return slice(i * ROWS, (i + 1) * ROWS)

    y_in = {}
    for j in range(1, N):
        y_in[j] = remote(
            ybuf.at[msg(j)], xbuf.at[j // 4, 0, msg(j % 4)], sent.at[0], ydr.at[j],
            (y - OFFS[j] + N) % N * N + z,
        )
        y_in[j].start()

    gather = {}

    def gather_one(s, m):
        h, i = m // 4, m % 4
        if s == 0 and m > 0:
            y_in[m].wait_recv()
        for d in range(2):
            if s > 0:
                gather[h, d, s - 1, i].wait_recv()
            if s == 3 and i not in FAR[d]:
                continue
            src = (N - s) % N if d == 0 else s
            dst = N - 1 - s if d == 0 else s + 1
            copy = remote(
                xbuf.at[h, src, msg(i)], xbuf.at[h, dst, msg(i)], sent.at[1],
                agr.at[h, d, s, i] if s < 3 else agl.at[h, d], side[d],
            )
            copy.start()
            gather[h, d, s, i] = copy

    def gather_last(h):
        for d in range(2):
            rows = xbuf.at[h, 4, FAR[d][0] * ROWS : (FAR[d][1] + 1) * ROWS]
            remote(rows, rows, sent.at[1], agl.at[h, d], side[d]).wait_recv()

    a, b = iota((4 * ROWS, 4 * ROWS), 0), iota((4 * ROWS, 4 * ROWS), 1)
    swap = jnp.where(
        (a // 16 == (b // 4) % 4) & ((a // 4) % 4 == b // 16) & (a % 4 == b % 4), 1.0, 0.0
    ).astype(BF16)

    def unfold(h, slot):
        rows = jnp.dot(swap, xbuf[h, slot], preferred_element_type=F32).astype(BF16)
        for q in range(FOLD):
            xrows[h, slot * ROWS : (slot + 1) * ROWS, q * wide : (q + 1) * wide] = rows[msg(q)]

    def hidden_of(h):
        gate_up = jnp.dot(xrows[h], w1[...], preferred_element_type=F32)
        gate = gate_up[:, :units]
        return (gate / (1.0 + jnp.exp(-gate)) * gate_up[:, units:]).astype(BF16)

    def down(h, hidden):
        for q in range(FOLD):
            part[h, q] = jnp.dot(
                hidden, w2[:, q * wide : (q + 1) * wide], preferred_element_type=F32
            )

    reduce = {}

    def place(d, s, q):
        return FAR[d].index(q) if s == 0 else 4 * s - 2 + q

    def reduce_stage(h, stage):
        for far in (True, False):
            s = stage if far else stage + 1
            if s > 3:
                continue
            for n in range(2):
                for d in range(2):
                    q = FAR[d if far else 1 - d][n]
                    slot = 4 - s if d == 0 else 4 + s
                    value = part[h, q, slot * ROWS : (slot + 1) * ROWS, :]
                    if stage > 0:
                        reduce[h, d, s - 1, q].wait_recv()
                        value = value + rbuf[h, d, place(d, s - 1, q)].astype(F32)
                    at = place(d, s, q)
                    sbuf[h, d, at] = value.astype(BF16)
                    copy = remote(
                        sbuf.at[h, d, at], rbuf.at[h, d, at], sent.at[2],
                        rsr.at[h, d, at] if s < 3 else rsl.at[h, d], side[d],
                    )
                    copy.start()
                    reduce[h, d, s, q] = copy

    def finish(h):
        for d in range(2):
            last = rbuf.at[h, d, 10:14]
            remote(last, last, sent.at[2], rsl.at[h, d], side[d]).wait_recv()
        sums = []
        for q in range(FOLD):
            value = part[h, q, 0:ROWS, :]
            for d in range(2):
                value = value + rbuf[h, d, 10 + q].astype(F32)
            sums.append(value.astype(BF16))
        folded = jnp.dot(
            swap, jnp.concatenate(sums, axis=0), preferred_element_type=F32
        ).astype(BF16)
        obuf[4 * h * ROWS : 4 * (h + 1) * ROWS] = folded
        for i in reversed(range(4)):
            j = h * 4 + i
            if j == 0:
                cbuf[0:ROWS, :] = folded[0:ROWS]
                continue
            remote(
                obuf.at[msg(j)], cbuf.at[msg(j)], sent.at[3], yrr.at[0],
                (y + OFFS[j] + N) % N * N + z,
            ).start()

    order = sorted(
        (Y_TIME[m] + 4.0 * s, m, s) for s in range(4) for m in range(N)
    )
    done = {}
    for _, m, s in order:
        gather_one(s, m)
        h = m // 4
        done[h, s] = done.get((h, s), 0) + 1
        if done[h, s] == 4:
            unfold(h, (N - s) % N)
            if s > 0:
                unfold(h, s)
    loads[0].wait()
    loads[1].wait()
    loads[2].wait()
    for h in range(2):
        gather_last(h)
        unfold(h, 4)
        hidden = hidden_of(h)
        down(h, hidden)
        reduce_stage(h, 0)
    for stage in range(1, 4):
        reduce_stage(0, stage)
        reduce_stage(1, stage)
    finish(0)
    finish(1)
    others = cbuf.at[ROWS : N * ROWS]
    remote(others, others, sent.at[3], yrr.at[0], right).wait_recv()
    both = jnp.dot(comb[...], cbuf[...], preferred_element_type=F32)
    half = both.shape[0] // 2
    result = both[:half] + both[half:]
    tok = out_ref.shape[0]
    for q in range(FOLD):
        out_ref[:, q * wide : (q + 1) * wide] = result[q * tok : (q + 1) * tok].astype(out_ref.dtype)
    for sem, whole in (
        (0, ybuf.at[ROWS : N * ROWS]), (1, xbuf.at[:, 0:7]), (2, sbuf), (3, obuf.at[ROWS : N * ROWS])
    ):
        remote(whole, whole, sent.at[sem], yrr.at[0], right).wait_send()


def body(tokens, expert_ids, gate_weights, replica_pick, placement, w_in, w_out):
    tok, width = tokens.shape
    units = w_out.shape[0]
    wide = width // FOLD
    vmem = pl.BlockSpec(memory_space=pltpu.VMEM)
    anywhere = pl.BlockSpec(memory_space=pl.ANY)
    dma = pltpu.SemaphoreType.DMA
    return pl.pallas_call(
        kernel,
        out_shape=jax.ShapeDtypeStruct((tok, width), BF16),
        in_specs=[vmem] * 5 + [anywhere] * 2,
        out_specs=vmem,
        scratch_shapes=[
            pltpu.VMEM((16, 128), F32),
            pltpu.VMEM((width, 2 * units), BF16),
            pltpu.VMEM((units, width), BF16),
            pltpu.VMEM((2 * FOLD * tok, 128), BF16),
            pltpu.VMEM((N * ROWS, wide), BF16),
            pltpu.VMEM((2, N, 4 * ROWS, wide), BF16),
            pltpu.VMEM((2, N * ROWS, width), BF16),
            pltpu.VMEM((2, FOLD, N * ROWS, wide), F32),
            pltpu.VMEM((2, 2, 14, ROWS, wide), BF16),
            pltpu.VMEM((2, 2, 14, ROWS, wide), BF16),
            pltpu.VMEM((N * ROWS, wide), BF16),
            pltpu.VMEM((N * ROWS, wide), BF16),
            dma((3,)),
            dma((4,)),
            dma((N,)),
            dma((2, 2, 3, 4)),
            dma((2, 2)),
            dma((2, 2, 10)),
            dma((2, 2)),
            dma((1,)),
        ],
        compiler_params=pltpu.CompilerParams(collective_id=0, has_side_effects=True),
    )(
        expert_ids.T, gate_weights.T, replica_pick.T, placement.reshape(1, -1),
        tokens, w_in, w_out,
    )


def solution(mesh):
    in_specs = (
        P(("dp", "expert"), None),
        P(("dp", "expert"), None),
        P(("dp", "expert"), None),
        P(("dp", "expert"), None),
        P(),
        P(None, None, "expert"),
        P("expert", None),
    )
    out_specs = P(("dp", "expert"), None)
    return jax.shard_map(body, mesh=mesh, in_specs=in_specs, out_specs=out_specs, check_vma=False)
```

```python
import functools

import jax
import jax.numpy as jnp
from jax import lax
from jax.experimental import pallas as pl
from jax.experimental.pallas import tpu as pltpu
from jax.sharding import PartitionSpec as P

N = 8
OFFS = (0, 1, -1, 2, -2, 3, -3, 4)
FOLD = 4
CAP = 4
ROWS = FOLD * CAP
MESH = pl.DeviceIdType.MESH
F32 = jnp.float32
BF16 = jnp.bfloat16
FAR = ((0, 1), (2, 3))
CHUNKS = ((0,), (1,), (2, 3), (4, 5), (6, 7))
ORDER = (
    (0, 0), (0, 1), (0, 2), (1, 0), (0, 3), (0, 4), (0, 5), (0, 6), (2, 0), (0, 7),
    (1, 1), (1, 2), (1, 3), (3, 0), (1, 4), (2, 1), (2, 3), (2, 2), (2, 4),
    (3, 3), (3, 4), (3, 1), (3, 2),
)
NEAR = (0, 1, 2, 3, 5, 6, 7)
VMEM_LIMIT = 32 * 1024 * 1024


def iota(shape, axis):
    return lax.broadcasted_iota(jnp.int32, shape, axis)


def routing(y, ids_ref, gw_ref, pick_ref, place_ref, pad):
    tok = ids_ref.shape[1]
    pad[...] = jnp.zeros_like(pad)
    pad[0:2, 0:tok] = ids_ref[...].astype(F32)
    pad[2:4, 0:tok] = pick_ref[...].astype(F32)
    pad[4:6, 0:tok] = gw_ref[...]
    pad[8:9, 0:N] = place_ref[...].astype(F32)
    wide = pad[0:8, :]
    wide = (
        wide
        + pltpu.roll(wide, tok, 1)
        + pltpu.roll(wide, 2 * tok, 1)
        + pltpu.roll(wide, 3 * tok, 1)
    )
    place_row = jnp.broadcast_to(pad[8:9, :], (N, 128))
    sub, lane = iota((N, 128), 0), iota((N, 128), 1)
    place_col = jnp.sum(jnp.where(sub == lane, place_row, 0.0), axis=1, keepdims=True)
    before = jnp.sum(
        jnp.where((place_row == place_col) & (lane < sub), 1.0, 0.0), axis=1, keepdims=True
    )
    subf = sub.astype(F32)
    row, col = iota((128, 128), 0), iota((128, 128), 1)
    j = row // ROWS
    offs = jnp.where(j % 2 == 1, (j + 1) // 2, -(j // 2))
    copy_of_row = ((y - offs + N) % N).astype(F32)
    chosen = []
    for k in range(2):
        match = place_col == wide[k : k + 1, :]
        copies = jnp.sum(jnp.where(match, 1.0, 0.0), axis=0, keepdims=True)
        wanted = jnp.where(copies > 1.5, wide[2 + k : 3 + k, :], 0.0)
        phys = jnp.sum(
            jnp.where(match & (before == wanted), subf, 0.0), axis=0, keepdims=True
        )
        chosen.append(jnp.where(copy_of_row == phys, 1.0, 0.0))
    earlier = jnp.where((row // tok == col // tok) & (row < col), 1.0, 0.0).astype(BF16)
    rank = jnp.dot((chosen[0] + chosen[1]).astype(BF16), earlier, preferred_element_type=F32)
    own = col // tok == (row // CAP) % FOLD
    slot = (row % CAP).astype(F32)
    in0 = jnp.where(own & (rank == slot), chosen[0], 0.0)
    in1 = jnp.where(own & (rank + chosen[0] == slot), chosen[1], 0.0)
    pick = (in0 + in1).astype(BF16)
    combine = in0 * wide[4:5, :] + in1 * wide[5:6, :]
    return pick, combine.T


def kernel(
    ids_hbm, gw_hbm, pick_hbm, place_hbm, tok_hbm, win_ref, wout_ref, out_ref,
    ids_ref, gw_ref, pick_ref, place_ref, tok_ref,
    pad, w1, w2, comb, ybuf, xbuf, xrows, xfar, part, pfar, sbuf, rbuf, obuf, cbuf, res,
    lsem, sent, ydr, agr, agl, rsr, rsl, yrr,
):
    wide = tok_ref.shape[1] // FOLD
    units = w2.shape[0]
    e = lax.axis_index("expert")
    y, z = e // N, e % N
    right = y * N + (z + 1) % N
    left = y * N + (z + N - 1) % N
    side = (right, left)

    barrier = pltpu.get_barrier_semaphore()
    peers = [(y + d) % N * N + z for d in (4, 3, 5, 2, 6, 1, 7)] + [right, left]
    for peer in peers:
        pl.semaphore_signal(barrier, inc=1, device_id={"expert": peer}, device_id_type=MESH)

    pairs = (
        (ids_hbm, ids_ref), (gw_hbm, gw_ref), (pick_hbm, pick_ref), (place_hbm, place_ref),
        (tok_hbm, tok_ref), (win_ref.at[0], w1.at[:, 0:units]),
        (win_ref.at[1], w1.at[:, units : 2 * units]), (wout_ref, w2),
    )
    loads = [pltpu.make_async_copy(src, dst, lsem.at[n]) for n, (src, dst) in enumerate(pairs)]
    for load in loads:
        load.start()
    for load in loads[:5]:
        load.wait()

    pick, combine = routing(y, ids_ref, gw_ref, pick_ref, place_ref, pad)
    tok_fold = jnp.concatenate(
        [tok_ref[:, q * wide : (q + 1) * wide] for q in range(FOLD)], axis=0
    )
    messages = jnp.dot(
        pick[:, : tok_fold.shape[0]], tok_fold, preferred_element_type=F32
    ).astype(BF16)
    ybuf[...] = messages
    xbuf[0, 0, 0:ROWS, :] = messages[0:ROWS]
    half_rows = combine[: tok_fold.shape[0]]
    high = half_rows.astype(BF16)
    comb[...] = jnp.concatenate([high, (half_rows - high.astype(F32)).astype(BF16)], axis=0)

    pl.semaphore_wait(barrier, len(peers))

    def remote(src, dst, send, recv, target):
        return pltpu.make_async_remote_copy(
            src_ref=src, dst_ref=dst, send_sem=send, recv_sem=recv,
            device_id={"expert": target}, device_id_type=MESH,
        )

    def msg(i, count=1):
        return slice(i * ROWS, (i + count) * ROWS)

    y_in = {}
    for j in range(1, N):
        y_in[j] = remote(
            ybuf.at[msg(j)], xbuf.at[j // 4, 0, msg(j % 4)], sent.at[0], ydr.at[j],
            (y - OFFS[j] + N) % N * N + z,
        )
        y_in[j].start()

    def hop(s, c, first, count, d):
        h, i = first // 4, first % 4
        src = (N - s) % N if d == 0 else s
        dst = N - 1 - s if d == 0 else s + 1
        return remote(
            xbuf.at[h, src, msg(i, count)], xbuf.at[h, dst, msg(i, count)], sent.at[1],
            agr.at[d, s, c] if s < 3 else agl.at[h, d], side[d],
        )

    def gather_one(s, n):
        if s == 0:
            if n > 0:
                y_in[n].wait_recv()
            chunk = [c for c in range(len(CHUNKS)) if n in CHUNKS[c]][0]
            for d in range(2):
                hop(0, chunk, n, 1, d).start()
            return
        first, count = CHUNKS[n][0], len(CHUNKS[n])
        for d in range(2):
            hop(s - 1, n, first, count, d).wait_recv()
            if s < 3 or first % 4 in FAR[d]:
                hop(s, n, first, count, d).start()

    def gather_last(h):
        for d in range(2):
            rows = xbuf.at[h, 4, msg(FAR[d][0], 2)]
            remote(rows, rows, sent.at[1], agl.at[h, d], side[d]).wait_recv()

    a, b = iota((4 * ROWS, 4 * ROWS), 0), iota((4 * ROWS, 4 * ROWS), 1)
    swap = jnp.where(
        (a // 16 == (b // 4) % 4) & ((a // 4) % 4 == b // 16) & (a % 4 == b % 4), 1.0, 0.0
    ).astype(BF16)

    def unfold(h, slot):
        rows = jnp.dot(swap, xbuf[h, slot], preferred_element_type=F32).astype(BF16)
        for q in range(FOLD):
            columns = slice(q * wide, (q + 1) * wide)
            if slot == 4:
                xfar[msg(h), columns] = rows[msg(q)]
            else:
                xrows[h, msg(NEAR.index(slot)), columns] = rows[msg(q)]

    def expert(rows, out):
        gate_up = jnp.dot(rows, w1[...], preferred_element_type=F32)
        gate = gate_up[:, :units]
        hidden = (gate / (1.0 + jnp.exp(-gate)) * gate_up[:, units:]).astype(BF16)
        for q in range(FOLD):
            out[q] = jnp.dot(
                hidden, w2[:, q * wide : (q + 1) * wide], preferred_element_type=F32
            )

    def partial_sum(h, slot, q):
        return pfar[q, msg(h), :] if slot == 4 else part[h, q, msg(NEAR.index(slot)), :]

    def ring(h, d, s, far):
        qs = FAR[d if far else 1 - d]
        at = 0 if s == 0 else 4 * s - 2 + qs[0]
        copy = remote(
            sbuf.at[h, d, at : at + 2], rbuf.at[h, d, at : at + 2], sent.at[2],
            rsl.at[h, d] if s == 3 else rsr.at[h, d, 2 * s - (0 if far else 1)], side[d],
        )
        return copy, at, qs

    def reduce_one(h, s, far):
        for d in range(2):
            copy, at, qs = ring(h, d, s, far)
            first = s == (0 if far else 1)
            if not first:
                arrived, back, _ = ring(h, d, s - 1, far)
                arrived.wait_recv()
            for n, q in enumerate(qs):
                value = partial_sum(h, 4 - s if d == 0 else 4 + s, q)
                if not first:
                    value = value + rbuf[h, d, back + n].astype(F32)
                sbuf[h, d, at + n] = value.astype(BF16)
            copy.start()

    def finish(h):
        for d in range(2):
            last = rbuf.at[h, d, 10:14]
            remote(last, last, sent.at[2], rsl.at[h, d], side[d]).wait_recv()
        sums = []
        for q in range(FOLD):
            value = partial_sum(h, 0, q)
            for d in range(2):
                value = value + rbuf[h, d, 10 + q].astype(F32)
            sums.append(value.astype(BF16))
        folded = jnp.dot(
            swap, jnp.concatenate(sums, axis=0), preferred_element_type=F32
        ).astype(BF16)
        obuf[msg(4 * h, 4)] = folded
        for i in reversed(range(4)):
            j = h * 4 + i
            if j == 0:
                cbuf[0:ROWS, :] = folded[0:ROWS]
                continue
            remote(
                obuf.at[msg(j)], cbuf.at[msg(j)], sent.at[3], yrr.at[0],
                (y + OFFS[j] + N) % N * N + z,
            ).start()

    waited = {}
    for s, n in ORDER:
        gather_one(s, n)
        h = n // 4 if s == 0 else CHUNKS[n][0] // 4
        waited[h, s] = waited.get((h, s), 0) + (1 if s == 0 else len(CHUNKS[n]))
        if waited[h, s] == 4:
            unfold(h, (N - s) % N)
            if s > 0:
                unfold(h, s)
    for load in loads[5:]:
        load.wait()
    for h in (1, 0):
        expert(xrows[h], part.at[h])
        reduce_one(h, 1, False)
    for h in (1, 0):
        gather_last(h)
        unfold(h, 4)
    expert(xfar[...], pfar)
    reduce_one(1, 0, True)
    reduce_one(0, 0, True)
    for s in range(1, 4):
        if s < 3:
            reduce_one(1, s + 1, False)
            reduce_one(0, s + 1, False)
        reduce_one(1, s, True)
        reduce_one(0, s, True)
    finish(1)
    finish(0)
    others = cbuf.at[ROWS : N * ROWS]
    remote(others, others, sent.at[3], yrr.at[0], right).wait_recv()
    both = jnp.dot(comb[...], cbuf[...], preferred_element_type=F32)
    half = both.shape[0] // 2
    result = both[:half] + both[half:]
    tok = tok_ref.shape[0]
    for q in range(FOLD):
        res[:, q * wide : (q + 1) * wide] = result[q * tok : (q + 1) * tok].astype(BF16)
    store = pltpu.make_async_copy(res, out_ref, lsem.at[0])
    store.start()
    for sem, whole in (
        (0, ybuf.at[ROWS : N * ROWS]), (1, xbuf.at[:, 0:7]), (2, sbuf), (3, obuf.at[ROWS : N * ROWS])
    ):
        remote(whole, whole, sent.at[sem], yrr.at[0], right).wait_send()
    store.wait()


def body(tokens, expert_ids, gate_weights, replica_pick, placement, w_in, w_out):
    tok, width = tokens.shape
    units = w_out.shape[0]
    wide = width // FOLD
    dma = pltpu.SemaphoreType.DMA
    operands = (
        expert_ids.T, gate_weights.T, replica_pick.T, placement.reshape(1, -1), tokens,
        w_in, w_out,
    )
    return pl.pallas_call(
        kernel,
        out_shape=jax.ShapeDtypeStruct((tok, width), BF16),
        in_specs=[pl.BlockSpec(memory_space=pl.ANY)] * 7,
        out_specs=pl.BlockSpec(memory_space=pl.ANY),
        scratch_shapes=[pltpu.VMEM(x.shape, x.dtype) for x in operands[:5]]
        + [
            pltpu.VMEM((16, 128), F32),
            pltpu.VMEM((width, 2 * units), BF16),
            pltpu.VMEM((units, width), BF16),
            pltpu.VMEM((2 * FOLD * tok, 128), BF16),
            pltpu.VMEM((N * ROWS, wide), BF16),
            pltpu.VMEM((2, N, 4 * ROWS, wide), BF16),
            pltpu.VMEM((2, 7 * ROWS, width), BF16),
            pltpu.VMEM((2 * ROWS, width), BF16),
            pltpu.VMEM((2, FOLD, 7 * ROWS, wide), F32),
            pltpu.VMEM((FOLD, 2 * ROWS, wide), F32),
            pltpu.VMEM((2, 2, 14, ROWS, wide), BF16),
            pltpu.VMEM((2, 2, 14, ROWS, wide), BF16),
            pltpu.VMEM((N * ROWS, wide), BF16),
            pltpu.VMEM((N * ROWS, wide), BF16),
            pltpu.VMEM((tok, width), BF16),
            dma((8,)),
            dma((4,)),
            dma((N,)),
            dma((2, 3, len(CHUNKS))),
            dma((2, 2)),
            dma((2, 2, 5)),
            dma((2, 2)),
            dma((1,)),
        ],
        compiler_params=pltpu.CompilerParams(
            collective_id=0, has_side_effects=True, vmem_limit_bytes=VMEM_LIMIT
        ),
    )(*[pltpu.with_memory_space_constraint(x, pltpu.HBM) for x in operands])


def solution(mesh):
    in_specs = (
        P(("dp", "expert"), None),
        P(("dp", "expert"), None),
        P(("dp", "expert"), None),
        P(("dp", "expert"), None),
        P(),
        P(None, None, "expert"),
        P("expert", None),
    )
    out_specs = P(("dp", "expert"), None)
    return jax.shard_map(body, mesh=mesh, in_specs=in_specs, out_specs=out_specs, check_vma=False)
```

```python
import functools

import jax
import jax.numpy as jnp
from jax import lax
from jax.experimental import pallas as pl
from jax.experimental.pallas import tpu as pltpu
from jax.sharding import PartitionSpec as P

N = 8
OFFS = (0, 1, -1, 2, -2, 3, -3, 4)
FOLD = 4
CAP = 4
ROWS = FOLD * CAP
MESH = pl.DeviceIdType.MESH
F32 = jnp.float32
BF16 = jnp.bfloat16
FAR = ((0, 1), (2, 3))
BOTH = (0, 1)
ORDER = (
    (0, 0, BOTH), (1, 0, BOTH), (0, 1, BOTH), (0, 2, BOTH), (0, 3, BOTH), (0, 4, BOTH),
    (0, 5, BOTH), (0, 6, BOTH), (0, 7, BOTH), (1, 1, BOTH),
    (1, 4, BOTH), (1, 5, BOTH), (1, 6, BOTH), (1, 7, BOTH), (1, 2, BOTH), (1, 3, BOTH),
    (2, 4, BOTH), (2, 5, BOTH), (2, 6, BOTH), (2, 7, BOTH),
    (2, 0, (0,)), (2, 2, (1,)), (2, 1, (0,)), (2, 3, (1,)),
    (3, 4, (0,)), (3, 6, (1,)), (3, 5, (0,)), (3, 7, (1,)),
    (2, 2, (0,)), (2, 0, (1,)), (2, 3, (0,)), (2, 1, (1,)),
    (3, 0, (0,)), (3, 2, (1,)), (3, 1, (0,)), (3, 3, (1,)),
)
VMEM_LIMIT = 32 * 1024 * 1024


def iota(shape, axis):
    return lax.broadcasted_iota(jnp.int32, shape, axis)


def routing(y, ids_ref, gw_ref, pick_ref, place_ref, pad):
    tok = ids_ref.shape[1]
    pad[...] = jnp.zeros_like(pad)
    pad[0:2, 0:tok] = ids_ref[...].astype(F32)
    pad[2:4, 0:tok] = pick_ref[...].astype(F32)
    pad[4:6, 0:tok] = gw_ref[...]
    pad[8:9, 0:N] = place_ref[...].astype(F32)
    wide = pad[0:8, :]
    wide = (
        wide
        + pltpu.roll(wide, tok, 1)
        + pltpu.roll(wide, 2 * tok, 1)
        + pltpu.roll(wide, 3 * tok, 1)
    )
    place_row = jnp.broadcast_to(pad[8:9, :], (N, 128))
    sub, lane = iota((N, 128), 0), iota((N, 128), 1)
    place_col = jnp.sum(jnp.where(sub == lane, place_row, 0.0), axis=1, keepdims=True)
    before = jnp.sum(
        jnp.where((place_row == place_col) & (lane < sub), 1.0, 0.0), axis=1, keepdims=True
    )
    subf = sub.astype(F32)
    row, col = iota((128, 128), 0), iota((128, 128), 1)
    j = row // ROWS
    offs = jnp.where(j % 2 == 1, (j + 1) // 2, -(j // 2))
    copy_of_row = ((y - offs + N) % N).astype(F32)
    chosen = []
    for k in range(2):
        match = place_col == wide[k : k + 1, :]
        copies = jnp.sum(jnp.where(match, 1.0, 0.0), axis=0, keepdims=True)
        wanted = jnp.where(copies > 1.5, wide[2 + k : 3 + k, :], 0.0)
        phys = jnp.sum(
            jnp.where(match & (before == wanted), subf, 0.0), axis=0, keepdims=True
        )
        chosen.append(jnp.where(copy_of_row == phys, 1.0, 0.0))
    earlier = jnp.where((row // tok == col // tok) & (row < col), 1.0, 0.0).astype(BF16)
    rank = jnp.dot((chosen[0] + chosen[1]).astype(BF16), earlier, preferred_element_type=F32)
    own = col // tok == (row // CAP) % FOLD
    slot = (row % CAP).astype(F32)
    in0 = jnp.where(own & (rank == slot), chosen[0], 0.0)
    in1 = jnp.where(own & (rank + chosen[0] == slot), chosen[1], 0.0)
    pick = (in0 + in1).astype(BF16)
    combine = in0 * wide[4:5, :] + in1 * wide[5:6, :]
    return pick, combine.T


def kernel(
    ids_hbm, gw_hbm, pick_hbm, place_hbm, tok_hbm, win_ref, wout_ref, out_ref,
    ids_ref, gw_ref, pick_ref, place_ref, tok_ref,
    pad, w1, w2, comb, ybuf, xbuf, xrows, part, sbuf, rbuf, obuf, cbuf, res,
    lsem, sent, ydr, agr, agl, rsr, rsl, yrr,
):
    wide = tok_ref.shape[1] // FOLD
    units = w2.shape[0]
    e = lax.axis_index("expert")
    y, z = e // N, e % N
    right = y * N + (z + 1) % N
    left = y * N + (z + N - 1) % N
    side = (right, left)

    barrier = pltpu.get_barrier_semaphore()
    peers = [(y + d) % N * N + z for d in (4, 3, 5, 2, 6, 1, 7)] + [right, left]
    for peer in peers:
        pl.semaphore_signal(barrier, inc=1, device_id={"expert": peer}, device_id_type=MESH)

    pairs = (
        (ids_hbm, ids_ref), (gw_hbm, gw_ref), (pick_hbm, pick_ref), (place_hbm, place_ref),
        (tok_hbm, tok_ref), (win_ref.at[0], w1.at[:, 0:units]),
        (win_ref.at[1], w1.at[:, units : 2 * units]), (wout_ref, w2),
    )
    loads = [pltpu.make_async_copy(src, dst, lsem.at[n]) for n, (src, dst) in enumerate(pairs)]
    for load in loads:
        load.start()
    for load in loads[:5]:
        load.wait()

    pick, combine = routing(y, ids_ref, gw_ref, pick_ref, place_ref, pad)
    tok_fold = jnp.concatenate(
        [tok_ref[:, q * wide : (q + 1) * wide] for q in range(FOLD)], axis=0
    )
    messages = jnp.dot(
        pick[:, : tok_fold.shape[0]], tok_fold, preferred_element_type=F32
    ).astype(BF16)
    ybuf[...] = messages
    xbuf[0, 0, 0:ROWS, :] = messages[0:ROWS]
    half_rows = combine[: tok_fold.shape[0]]
    high = half_rows.astype(BF16)
    comb[...] = jnp.concatenate([high, (half_rows - high.astype(F32)).astype(BF16)], axis=0)

    pl.semaphore_wait(barrier, len(peers))

    def remote(src, dst, send, recv, target):
        return pltpu.make_async_remote_copy(
            src_ref=src, dst_ref=dst, send_sem=send, recv_sem=recv,
            device_id={"expert": target}, device_id_type=MESH,
        )

    def msg(i, count=1):
        return slice(i * ROWS, (i + count) * ROWS)

    y_in = {}
    for j in range(1, N):
        y_in[j] = remote(
            ybuf.at[msg(j)], xbuf.at[j // 4, 0, msg(j % 4)], sent.at[0], ydr.at[j],
            (y - OFFS[j] + N) % N * N + z,
        )
        y_in[j].start()

    def hop(s, m, d):
        h, i = m // 4, m % 4
        src = (N - s) % N if d == 0 else s
        dst = N - 1 - s if d == 0 else s + 1
        if s < 2:
            arrival = agr.at[d, 8 * s + m]
        elif s == 2 and i in FAR[d]:
            arrival = agr.at[d, 16 + 2 * h + i % 2]
        else:
            arrival = agl.at[h, d, s - 2]
        return remote(
            xbuf.at[h, src, msg(i)], xbuf.at[h, dst, msg(i)], sent.at[1], arrival, side[d]
        )

    def gather_one(s, m, d):
        if s > 0:
            hop(s - 1, m, d).wait_recv()
        hop(s, m, d).start()

    def gather_last(h):
        for d in range(2):
            for slot, first in ((5 - 2 * d, FAR[1 - d][0]), (4, FAR[d][0])):
                rows = xbuf.at[h, slot, msg(first, 2)]
                remote(
                    rows, rows, sent.at[1], agl.at[h, d, 1 if slot == 4 else 0], side[d]
                ).wait_recv()

    a, b = iota((4 * ROWS, 4 * ROWS), 0), iota((4 * ROWS, 4 * ROWS), 1)
    swap = jnp.where(
        (a // 16 == (b // 4) % 4) & ((a // 4) % 4 == b // 16) & (a % 4 == b % 4), 1.0, 0.0
    ).astype(BF16)

    def unfold(h, slot):
        rows = jnp.dot(swap, xbuf[h, slot], preferred_element_type=F32).astype(BF16)
        for q in range(FOLD):
            xrows[h, msg(slot), q * wide : (q + 1) * wide] = rows[msg(q)]

    def expert(rows, out):
        gate_up = jnp.dot(rows, w1[...], preferred_element_type=F32)
        gate = gate_up[:, :units]
        hidden = (gate / (1.0 + jnp.exp(-gate)) * gate_up[:, units:]).astype(BF16)
        for q in range(FOLD):
            out[q] = jnp.dot(
                hidden, w2[:, q * wide : (q + 1) * wide], preferred_element_type=F32
            )

    def ring(h, d, s, q):
        at = FAR[d].index(q) if s == 0 else 4 * s - 2 + q
        copy = remote(
            sbuf.at[h, d, at], rbuf.at[h, d, at], sent.at[2],
            rsl.at[h, d] if s == 3 else rsr.at[h, d, at], side[d],
        )
        return copy, at

    def reduce_stage(h, stage):
        for far in (True, False):
            s = stage if far else stage + 1
            if s > 3:
                continue
            for n in range(2):
                for d in range(2):
                    q = FAR[d if far else 1 - d][n]
                    slot = 4 - s if d == 0 else 4 + s
                    value = part[h, q, msg(slot), :]
                    if stage > 0:
                        arrived, back = ring(h, d, s - 1, q)
                        arrived.wait_recv()
                        value = value + rbuf[h, d, back].astype(F32)
                    copy, at = ring(h, d, s, q)
                    sbuf[h, d, at] = value.astype(BF16)
                    copy.start()

    def finish(h):
        for d in range(2):
            last = rbuf.at[h, d, 10:14]
            remote(last, last, sent.at[2], rsl.at[h, d], side[d]).wait_recv()
        sums = []
        for q in range(FOLD):
            value = part[h, q, 0:ROWS, :]
            for d in range(2):
                value = value + rbuf[h, d, 10 + q].astype(F32)
            sums.append(value.astype(BF16))
        folded = jnp.dot(
            swap, jnp.concatenate(sums, axis=0), preferred_element_type=F32
        ).astype(BF16)
        obuf[msg(4 * h, 4)] = folded
        for i in reversed(range(4)):
            j = h * 4 + i
            if j == 0:
                cbuf[0:ROWS, :] = folded[0:ROWS]
                continue
            remote(
                obuf.at[msg(j)], cbuf.at[msg(j)], sent.at[3], yrr.at[0],
                (y + OFFS[j] + N) % N * N + z,
            ).start()

    waited = {}
    for s, m, directions in ORDER:
        if s == 0 and m > 0:
            y_in[m].wait_recv()
        for d in directions:
            gather_one(s, m, d)
            if s == 0 and d == 1:
                continue
            key = m // 4, (N - s) % N if d == 0 else s
            waited[key] = waited.get(key, 0) + 1
            if waited[key] == 4:
                unfold(*key)
    for load in loads[5:]:
        load.wait()
    for h in (1, 0):
        gather_last(h)
        for slot in (5, 3, 4):
            unfold(h, slot)
        expert(xrows[h], part.at[h])
        reduce_stage(h, 0)
    for stage in range(1, 4):
        reduce_stage(1, stage)
        reduce_stage(0, stage)
    finish(1)
    finish(0)
    others = cbuf.at[ROWS : N * ROWS]
    remote(others, others, sent.at[3], yrr.at[0], right).wait_recv()
    both = jnp.dot(comb[...], cbuf[...], preferred_element_type=F32)
    half = both.shape[0] // 2
    result = both[:half] + both[half:]
    tok = tok_ref.shape[0]
    for q in range(FOLD):
        res[:, q * wide : (q + 1) * wide] = result[q * tok : (q + 1) * tok].astype(BF16)
    store = pltpu.make_async_copy(res, out_ref, lsem.at[0])
    store.start()
    for sem, whole in (
        (0, ybuf.at[ROWS : N * ROWS]), (1, xbuf.at[:, 0:7]), (2, sbuf), (3, obuf.at[ROWS : N * ROWS])
    ):
        remote(whole, whole, sent.at[sem], yrr.at[0], right).wait_send()
    store.wait()


def body(tokens, expert_ids, gate_weights, replica_pick, placement, w_in, w_out):
    tok, width = tokens.shape
    units = w_out.shape[0]
    wide = width // FOLD
    dma = pltpu.SemaphoreType.DMA
    operands = (
        expert_ids.T, gate_weights.T, replica_pick.T, placement.reshape(1, -1), tokens,
        w_in, w_out,
    )
    return pl.pallas_call(
        kernel,
        out_shape=jax.ShapeDtypeStruct((tok, width), BF16),
        in_specs=[pl.BlockSpec(memory_space=pl.ANY)] * 7,
        out_specs=pl.BlockSpec(memory_space=pl.ANY),
        scratch_shapes=[pltpu.VMEM(x.shape, x.dtype) for x in operands[:5]]
        + [
            pltpu.VMEM((16, 128), F32),
            pltpu.VMEM((width, 2 * units), BF16),
            pltpu.VMEM((units, width), BF16),
            pltpu.VMEM((2 * FOLD * tok, 128), BF16),
            pltpu.VMEM((N * ROWS, wide), BF16),
            pltpu.VMEM((2, N, 4 * ROWS, wide), BF16),
            pltpu.VMEM((2, N * ROWS, width), BF16),
            pltpu.VMEM((2, FOLD, N * ROWS, wide), F32),
            pltpu.VMEM((2, 2, 14, ROWS, wide), BF16),
            pltpu.VMEM((2, 2, 14, ROWS, wide), BF16),
            pltpu.VMEM((N * ROWS, wide), BF16),
            pltpu.VMEM((N * ROWS, wide), BF16),
            pltpu.VMEM((tok, width), BF16),
            dma((8,)),
            dma((4,)),
            dma((N,)),
            dma((2, 20)),
            dma((2, 2, 2)),
            dma((2, 2, 10)),
            dma((2, 2)),
            dma((1,)),
        ],
        compiler_params=pltpu.CompilerParams(
            collective_id=0, has_side_effects=True, vmem_limit_bytes=VMEM_LIMIT
        ),
    )(*[pltpu.with_memory_space_constraint(x, pltpu.HBM) for x in operands])


def solution(mesh):
    in_specs = (
        P(("dp", "expert"), None),
        P(("dp", "expert"), None),
        P(("dp", "expert"), None),
        P(("dp", "expert"), None),
        P(),
        P(None, None, "expert"),
        P("expert", None),
    )
    out_specs = P(("dp", "expert"), None)
    return jax.shard_map(body, mesh=mesh, in_specs=in_specs, out_specs=out_specs, check_vma=False)
```

```python
import jax
import jax.numpy as jnp
from jax import lax
from jax.experimental import pallas as pl
from jax.experimental.pallas import tpu as pltpu
from jax.sharding import PartitionSpec as P

N = 8
OFFS = (0, 1, -1, 2, -2, 3, -3, 4)
FOLD = 4
CAP = 4
ROWS = FOLD * CAP
MESH = pl.DeviceIdType.MESH
F32 = jnp.float32
BF16 = jnp.bfloat16
FAR = ((0, 1), (2, 3))
RELAY, ARRIVED, HIDDEN, DOWN, SUM, FINISH = range(6)
PROGRAM = (
    (RELAY, 0, 0, 0), (RELAY, 0, 0, 1), (RELAY, 0, 1, 0), (RELAY, 0, 1, 1), (RELAY, 0, 2, 0),
    (RELAY, 0, 2, 1), (RELAY, 1, 0, 1), (RELAY, 1, 0, 0), (RELAY, 0, 3, 0), (RELAY, 0, 3, 1),
    (RELAY, 0, 4, 0), (RELAY, 0, 4, 1), (RELAY, 0, 5, 0), (RELAY, 0, 5, 1), (RELAY, 1, 1, 0),
    (RELAY, 1, 1, 1), (RELAY, 0, 7, 0), (RELAY, 0, 7, 1), (RELAY, 1, 2, 0), (RELAY, 0, 6, 0),
    (RELAY, 0, 6, 1), (RELAY, 1, 2, 1), (RELAY, 1, 4, 0), (RELAY, 1, 3, 1), (RELAY, 2, 0, 0),
    (RELAY, 1, 5, 0), (RELAY, 1, 4, 1), (RELAY, 2, 0, 1), (RELAY, 1, 7, 1), (RELAY, 1, 3, 0),
    (RELAY, 2, 1, 0), (RELAY, 1, 7, 0), (RELAY, 1, 6, 1), (RELAY, 2, 2, 1), (RELAY, 2, 3, 1),
    (RELAY, 2, 4, 0), (RELAY, 1, 5, 1), (RELAY, 1, 6, 0), (RELAY, 2, 2, 0), (RELAY, 2, 5, 0),
    (RELAY, 2, 1, 1), (RELAY, 2, 7, 1), (RELAY, 2, 6, 1), (RELAY, 3, 0, 0), (RELAY, 2, 3, 0),
    (RELAY, 3, 2, 1), (RELAY, 3, 3, 1), (RELAY, 3, 1, 0), (RELAY, 2, 5, 1), (RELAY, 2, 6, 0),
    (RELAY, 3, 4, 0), (RELAY, 2, 7, 0), (RELAY, 2, 4, 1), (RELAY, 3, 7, 1), (RELAY, 3, 5, 0),
    (RELAY, 3, 6, 1), (ARRIVED, 0), (HIDDEN, 0), (DOWN, 0), (SUM, 0, 2, 1), (SUM, 0, 1, 0),
    (SUM, 1, 3, 0), (SUM, 1, 1, 1), (SUM, 1, 0, 1), (SUM, 0, 0, 0), (SUM, 1, 2, 0), (SUM, 0, 3, 1),
    (ARRIVED, 1), (HIDDEN, 1), (DOWN, 1), (SUM, 0, 7, 1), (SUM, 0, 4, 0), (SUM, 0, 5, 0),
    (SUM, 0, 6, 1), (SUM, 1, 7, 0), (SUM, 1, 2, 1), (SUM, 1, 6, 0), (SUM, 1, 1, 0), (SUM, 2, 1, 1),
    (SUM, 2, 3, 0), (SUM, 1, 4, 1), (SUM, 1, 5, 1), (SUM, 1, 7, 1), (SUM, 1, 4, 0), (SUM, 1, 3, 1),
    (SUM, 1, 5, 0), (SUM, 2, 2, 0), (SUM, 1, 6, 1), (SUM, 2, 2, 1), (SUM, 1, 0, 0), (SUM, 2, 7, 0),
    (SUM, 2, 1, 0), (SUM, 2, 4, 1), (SUM, 2, 6, 0), (SUM, 3, 3, 0), (SUM, 2, 5, 1), (SUM, 2, 7, 1),
    (SUM, 2, 3, 1), (SUM, 2, 6, 1), (SUM, 2, 5, 0), (SUM, 3, 2, 1), (SUM, 2, 4, 0), (SUM, 2, 0, 0),
    (SUM, 3, 4, 1), (SUM, 3, 5, 1), (SUM, 3, 7, 0), (SUM, 3, 7, 1), (SUM, 3, 6, 0), (SUM, 3, 2, 0),
    (SUM, 3, 3, 1), (SUM, 3, 6, 1), (SUM, 3, 5, 0), (SUM, 3, 4, 0), (SUM, 3, 1, 0), (SUM, 2, 0, 1),
    (SUM, 3, 1, 1), (FINISH, 7), (SUM, 3, 0, 0), (FINISH, 6), (FINISH, 5), (SUM, 3, 0, 1),
    (FINISH, 4), (FINISH, 2), (FINISH, 3), (FINISH, 1), (FINISH, 0),
)
VMEM_LIMIT = 32 * 1024 * 1024


def iota(shape, axis):
    return lax.broadcasted_iota(jnp.int32, shape, axis)


def routing(y, ids_ref, gw_ref, pick_ref, place_ref, pad):
    tok = ids_ref.shape[1]
    pad[...] = jnp.zeros_like(pad)
    pad[0:2, 0:tok] = ids_ref[...].astype(F32)
    pad[2:4, 0:tok] = pick_ref[...].astype(F32)
    pad[4:6, 0:tok] = gw_ref[...]
    pad[8:9, 0:N] = place_ref[...].astype(F32)
    wide = pad[0:8, :]
    wide = (
        wide
        + pltpu.roll(wide, tok, 1)
        + pltpu.roll(wide, 2 * tok, 1)
        + pltpu.roll(wide, 3 * tok, 1)
    )
    place_row = jnp.broadcast_to(pad[8:9, :], (N, 128))
    sub, lane = iota((N, 128), 0), iota((N, 128), 1)
    place_col = jnp.sum(jnp.where(sub == lane, place_row, 0.0), axis=1, keepdims=True)
    before = jnp.sum(
        jnp.where((place_row == place_col) & (lane < sub), 1.0, 0.0), axis=1, keepdims=True
    )
    subf = sub.astype(F32)
    row, col = iota((128, 128), 0), iota((128, 128), 1)
    j = row // ROWS
    offs = jnp.where(j % 2 == 1, (j + 1) // 2, -(j // 2))
    copy_of_row = ((y - offs + N) % N).astype(F32)
    chosen = []
    for k in range(2):
        match = place_col == wide[k : k + 1, :]
        copies = jnp.sum(jnp.where(match, 1.0, 0.0), axis=0, keepdims=True)
        wanted = jnp.where(copies > 1.5, wide[2 + k : 3 + k, :], 0.0)
        phys = jnp.sum(
            jnp.where(match & (before == wanted), subf, 0.0), axis=0, keepdims=True
        )
        chosen.append(jnp.where(copy_of_row == phys, 1.0, 0.0))
    earlier = jnp.where((row // tok == col // tok) & (row < col), 1.0, 0.0).astype(BF16)
    rank = jnp.dot((chosen[0] + chosen[1]).astype(BF16), earlier, preferred_element_type=F32)
    own = col // tok == (row // CAP) % FOLD
    slot = (row % CAP).astype(F32)
    in0 = jnp.where(own & (rank == slot), chosen[0], 0.0)
    in1 = jnp.where(own & (rank + chosen[0] == slot), chosen[1], 0.0)
    pick = (in0 + in1).astype(BF16)
    combine = in0 * wide[4:5, :] + in1 * wide[5:6, :]
    return pick, combine.T


def kernel(
    ids_hbm, gw_hbm, pick_hbm, place_hbm, tok_hbm, win_ref, wout_ref, out_ref,
    ids_ref, gw_ref, pick_ref, place_ref, tok_ref,
    pad, w1, w2, comb, ybuf, xbuf, xrows, part, sbuf, rbuf, obuf, cbuf, res,
    lsem, sent, ydr, agr, agl, rsr, yrr,
):
    wide = tok_ref.shape[1] // FOLD
    units = wout_ref.shape[0]
    e = lax.axis_index("expert")
    y, z = e // N, e % N
    right = y * N + (z + 1) % N
    left = y * N + (z + N - 1) % N
    side = (right, left)

    barrier = pltpu.get_barrier_semaphore()
    peers = [(y + d) % N * N + z for d in (4, 3, 5, 2, 6, 1, 7)] + [right, left]
    for peer in peers:
        pl.semaphore_signal(barrier, inc=1, device_id={"expert": peer}, device_id_type=MESH)

    pairs = (
        (ids_hbm, ids_ref), (gw_hbm, gw_ref), (pick_hbm, pick_ref), (place_hbm, place_ref),
        (tok_hbm, tok_ref), (win_ref.at[0], w1.at[:, 0:units]),
        (win_ref.at[1], w1.at[:, units : 2 * units]),
    ) + tuple(
        (wout_ref.at[:, q * wide : (q + 1) * wide], w2.at[q // 2, q % 2 * units : (q % 2 + 1) * units])
        for q in range(FOLD)
    )
    loads = [pltpu.make_async_copy(src, dst, lsem.at[n]) for n, (src, dst) in enumerate(pairs)]
    for load in loads:
        load.start()
    for load in loads[:5]:
        load.wait()

    pick, combine = routing(y, ids_ref, gw_ref, pick_ref, place_ref, pad)
    tok_fold = jnp.concatenate(
        [tok_ref[:, q * wide : (q + 1) * wide] for q in range(FOLD)], axis=0
    )
    messages = jnp.dot(
        pick[:, : tok_fold.shape[0]], tok_fold, preferred_element_type=F32
    ).astype(BF16)
    ybuf[...] = messages
    xbuf[0, 0, 0:ROWS, :] = messages[0:ROWS]
    half_rows = combine[: tok_fold.shape[0]]
    high = half_rows.astype(BF16)
    comb[...] = jnp.concatenate([high, (half_rows - high.astype(F32)).astype(BF16)], axis=0)

    pl.semaphore_wait(barrier, len(peers))

    def remote(src, dst, send, recv, target):
        return pltpu.make_async_remote_copy(
            src_ref=src, dst_ref=dst, send_sem=send, recv_sem=recv,
            device_id={"expert": target}, device_id_type=MESH,
        )

    def msg(i, count=1):
        return slice(i * ROWS, (i + count) * ROWS)

    y_in = {}
    for j in range(1, N):
        y_in[j] = remote(
            ybuf.at[msg(j)], xbuf.at[j // 4, 0, msg(j % 4)], sent.at[0], ydr.at[j],
            (y - OFFS[j] + N) % N * N + z,
        )
        y_in[j].start()

    def hop(s, m, d):
        h, i = m // 4, m % 4
        src = (N - s) % N if d == 0 else s
        dst = N - 1 - s if d == 0 else s + 1
        if s < 2:
            arrival = agr.at[d, 8 * s + m]
        elif s == 2 and i in FAR[d]:
            arrival = agr.at[d, 16 + 2 * h + i % 2]
        else:
            arrival = agl.at[h, d, s - 2]
        return remote(
            xbuf.at[h, src, msg(i)], xbuf.at[h, dst, msg(i)], sent.at[1], arrival, side[d]
        )

    waited = {}

    def relay(s, m, d):
        if s > 0:
            hop(s - 1, m, d).wait_recv()
        elif d == 0 and m > 0:
            y_in[m].wait_recv()
        hop(s, m, d).start()
        if s > 0 or d == 0:
            key = m // 4, (N - s) % N if d == 0 else s
            waited[key] = waited.get(key, 0) + 1
            if waited[key] == 4:
                unfold(*key)

    def arrived(h):
        for d in range(2):
            for slot, first in ((5 - 2 * d, FAR[1 - d][0]), (4, FAR[d][0])):
                rows = xbuf.at[h, slot, msg(first, 2)]
                remote(
                    rows, rows, sent.at[1], agl.at[h, d, 1 if slot == 4 else 0], side[d]
                ).wait_recv()
        for slot in (5, 3, 4):
            unfold(h, slot)

    a, b = iota((4 * ROWS, 4 * ROWS), 0), iota((4 * ROWS, 4 * ROWS), 1)
    swap = jnp.where(
        (a // 16 == (b // 4) % 4) & ((a // 4) % 4 == b // 16) & (a % 4 == b % 4), 1.0, 0.0
    ).astype(BF16)

    def unfold(h, slot):
        rows = jnp.dot(swap, xbuf[h, slot], preferred_element_type=F32).astype(BF16)
        for q in range(FOLD):
            xrows[h, msg(slot), q * wide : (q + 1) * wide] = rows[msg(q)]

    hidden = {}

    def hidden_of(h):
        gate_up = jnp.dot(xrows[h], w1[...], preferred_element_type=F32)
        gate = gate_up[:, :units]
        act = (gate / (1.0 + jnp.exp(-gate)) * gate_up[:, units:]).astype(BF16)
        rows = act.shape[0]
        r, c = iota((2 * rows, rows), 0), iota((2 * rows, rows), 1)
        twice = jnp.where((r // 8 == c // 4) & (r % 4 == c % 4), 1.0, 0.0).astype(BF16)
        spread = jnp.dot(twice, act, preferred_element_type=F32)
        odd = iota(spread.shape, 0) // 4 % 2 == 1
        hidden[h] = jnp.concatenate(
            [jnp.where(odd, 0.0, spread), jnp.where(odd, spread, 0.0)], axis=1
        ).astype(BF16)

    def down(h):
        for pair in range(2):
            part[h, pair] = jnp.dot(hidden[h], w2[pair], preferred_element_type=F32)

    def partial_sum(m, slot):
        rows = slice(32 * slot + 8 * (m % 4), 32 * slot + 8 * (m % 4) + 8)
        return jnp.concatenate([part[m // 4, 0, rows, :], part[m // 4, 1, rows, :]], axis=0)

    def ring(d, s, m):
        if m % 4 in FAR[d]:
            at = 4 * s + 2 * (m // 4) + m % 2
        else:
            at = 12 + 4 * s + 2 * (m // 4) + m % 2
        copy = remote(
            sbuf.at[d, at], rbuf.at[d, at], sent.at[2], rsr.at[d, at], side[d]
        )
        return copy, at

    def add_on(s, m, d):
        value = partial_sum(m, 4 - s if d == 0 else 4 + s)
        if s > (0 if m % 4 in FAR[d] else 1):
            earlier, at = ring(d, s - 1, m)
            earlier.wait_recv()
            value = value + rbuf[d, at].astype(F32)
        copy, at = ring(d, s, m)
        sbuf[d, at] = value.astype(BF16)
        copy.start()

    def finish(m):
        value = partial_sum(m, 0)
        for d in range(2):
            last, at = ring(d, 3, m)
            last.wait_recv()
            value = value + rbuf[d, at].astype(F32)
        if m == 0:
            cbuf[0:ROWS, :] = value.astype(BF16)
            return
        obuf[msg(m)] = value.astype(BF16)
        remote(
            obuf.at[msg(m)], cbuf.at[msg(m)], sent.at[3], yrr.at[0],
            (y + OFFS[m] + N) % N * N + z,
        ).start()

    steps = {
        RELAY: relay, ARRIVED: arrived, HIDDEN: hidden_of, DOWN: down, SUM: add_on, FINISH: finish
    }
    for kind, *which in PROGRAM:
        if kind == HIDDEN and not hidden:
            for load in loads[5:]:
                load.wait()
        steps[kind](*which)
    others = cbuf.at[ROWS : N * ROWS]
    remote(others, others, sent.at[3], yrr.at[0], right).wait_recv()
    both = jnp.dot(comb[...], cbuf[...], preferred_element_type=F32)
    half = both.shape[0] // 2
    result = both[:half] + both[half:]
    tok = tok_ref.shape[0]
    for q in range(FOLD):
        res[:, q * wide : (q + 1) * wide] = result[q * tok : (q + 1) * tok].astype(BF16)
    store = pltpu.make_async_copy(res, out_ref, lsem.at[0])
    store.start()
    for sem, whole in (
        (0, ybuf.at[ROWS : N * ROWS]), (1, xbuf.at[:, 0:7]), (2, sbuf), (3, obuf.at[ROWS : N * ROWS])
    ):
        remote(whole, whole, sent.at[sem], yrr.at[0], right).wait_send()
    store.wait()


def body(tokens, expert_ids, gate_weights, replica_pick, placement, w_in, w_out):
    tok, width = tokens.shape
    units = w_out.shape[0]
    wide = width // FOLD
    dma = pltpu.SemaphoreType.DMA
    operands = (
        expert_ids.T, gate_weights.T, replica_pick.T, placement.reshape(1, -1), tokens,
        w_in, w_out,
    )
    return pl.pallas_call(
        kernel,
        out_shape=jax.ShapeDtypeStruct((tok, width), BF16),
        in_specs=[pl.BlockSpec(memory_space=pl.ANY)] * 7,
        out_specs=pl.BlockSpec(memory_space=pl.ANY),
        scratch_shapes=[pltpu.VMEM(x.shape, x.dtype) for x in operands[:5]]
        + [
            pltpu.VMEM((16, 128), F32),
            pltpu.VMEM((width, 2 * units), BF16),
            pltpu.VMEM((2, 2 * units, wide), BF16),
            pltpu.VMEM((2 * FOLD * tok, 128), BF16),
            pltpu.VMEM((N * ROWS, wide), BF16),
            pltpu.VMEM((2, N, 4 * ROWS, wide), BF16),
            pltpu.VMEM((2, N * ROWS, width), BF16),
            pltpu.VMEM((2, 2, 2 * N * ROWS, wide), F32),
            pltpu.VMEM((2, 28, ROWS, wide), BF16),
            pltpu.VMEM((2, 28, ROWS, wide), BF16),
            pltpu.VMEM((N * ROWS, wide), BF16),
            pltpu.VMEM((N * ROWS, wide), BF16),
            pltpu.VMEM((tok, width), BF16),
            dma((11,)),
            dma((4,)),
            dma((N,)),
            dma((2, 20)),
            dma((2, 2, 2)),
            dma((2, 28)),
            dma((1,)),
        ],
        compiler_params=pltpu.CompilerParams(
            collective_id=0, has_side_effects=True, vmem_limit_bytes=VMEM_LIMIT
        ),
    )(*[pltpu.with_memory_space_constraint(x, pltpu.HBM) for x in operands])


def solution(mesh):
    in_specs = (
        P(("dp", "expert"), None),
        P(("dp", "expert"), None),
        P(("dp", "expert"), None),
        P(("dp", "expert"), None),
        P(),
        P(None, None, "expert"),
        P("expert", None),
    )
    out_specs = P(("dp", "expert"), None)
    return jax.shard_map(body, mesh=mesh, in_specs=in_specs, out_specs=out_specs, check_vma=False)
```

```python
import jax
import jax.numpy as jnp
from jax import lax
from jax.experimental import pallas as pl
from jax.experimental.pallas import tpu as pltpu
from jax.sharding import PartitionSpec as P

N = 8
OFFS = (0, 1, -1, 2, -2, 3, -3, 4)
FOLD = 4
CAP = 4
ROWS = FOLD * CAP
MESH = pl.DeviceIdType.MESH
F32 = jnp.float32
BF16 = jnp.bfloat16
FAR = ((0, 1), (2, 3))
RELAY, ARRIVED, EARLY, LATE, SUM, FINISH = range(6)
PROGRAM = (
    (RELAY, 0, 0, 0), (RELAY, 0, 0, 1), (RELAY, 0, 1, 0), (RELAY, 0, 1, 1), (RELAY, 0, 2, 0),
    (RELAY, 0, 2, 1), (RELAY, 1, 0, 1), (RELAY, 1, 0, 0), (RELAY, 0, 3, 0), (RELAY, 0, 3, 1),
    (RELAY, 0, 4, 0), (RELAY, 0, 4, 1), (RELAY, 0, 5, 0), (RELAY, 0, 5, 1), (RELAY, 1, 1, 0),
    (RELAY, 1, 1, 1), (RELAY, 0, 7, 0), (RELAY, 0, 7, 1), (RELAY, 1, 2, 0), (RELAY, 0, 6, 0),
    (RELAY, 0, 6, 1), (RELAY, 1, 2, 1), (RELAY, 1, 4, 0), (RELAY, 1, 3, 1), (RELAY, 2, 0, 0),
    (RELAY, 1, 5, 0), (RELAY, 1, 4, 1), (RELAY, 2, 0, 1), (RELAY, 1, 7, 1), (RELAY, 1, 3, 0),
    (RELAY, 2, 1, 0), (RELAY, 1, 7, 0), (RELAY, 1, 6, 1), (RELAY, 2, 2, 1), (RELAY, 2, 3, 1),
    (RELAY, 2, 4, 0), (RELAY, 1, 5, 1), (RELAY, 1, 6, 0), (RELAY, 2, 2, 0), (RELAY, 2, 5, 0),
    (RELAY, 2, 1, 1), (RELAY, 2, 7, 1), (RELAY, 2, 6, 1), (RELAY, 3, 0, 0), (RELAY, 2, 3, 0),
    (RELAY, 3, 2, 1), (RELAY, 3, 3, 1), (RELAY, 3, 1, 0), (RELAY, 2, 5, 1), (RELAY, 2, 6, 0),
    (RELAY, 3, 4, 0), (RELAY, 2, 7, 0), (RELAY, 2, 4, 1), (RELAY, 3, 7, 1), (RELAY, 3, 5, 0),
    (RELAY, 3, 6, 1), (EARLY, 0), (ARRIVED, 0), (LATE, 0), (SUM, 0, 2, 1), (SUM, 0, 1, 0),
    (SUM, 1, 3, 0), (SUM, 1, 1, 1), (SUM, 1, 0, 1), (SUM, 0, 0, 0), (SUM, 1, 2, 0), (SUM, 0, 3, 1),
    (EARLY, 1), (ARRIVED, 1), (LATE, 1), (SUM, 0, 7, 1), (SUM, 0, 4, 0), (SUM, 0, 5, 0),
    (SUM, 0, 6, 1), (SUM, 1, 7, 0), (SUM, 1, 2, 1), (SUM, 1, 6, 0), (SUM, 1, 1, 0), (SUM, 2, 1, 1),
    (SUM, 2, 3, 0), (SUM, 1, 4, 1), (SUM, 1, 5, 1), (SUM, 1, 7, 1), (SUM, 1, 4, 0), (SUM, 1, 3, 1),
    (SUM, 1, 5, 0), (SUM, 2, 2, 0), (SUM, 1, 6, 1), (SUM, 2, 2, 1), (SUM, 1, 0, 0), (SUM, 2, 7, 0),
    (SUM, 2, 1, 0), (SUM, 2, 4, 1), (SUM, 2, 6, 0), (SUM, 3, 3, 0), (SUM, 2, 5, 1), (SUM, 2, 7, 1),
    (SUM, 2, 3, 1), (SUM, 2, 6, 1), (SUM, 2, 5, 0), (SUM, 3, 2, 1), (SUM, 2, 4, 0), (SUM, 2, 0, 0),
    (SUM, 3, 4, 1), (SUM, 3, 5, 1), (SUM, 3, 7, 0), (SUM, 3, 7, 1), (SUM, 3, 6, 0), (SUM, 3, 2, 0),
    (SUM, 3, 3, 1), (SUM, 3, 6, 1), (SUM, 3, 5, 0), (SUM, 3, 4, 0), (SUM, 3, 1, 0), (SUM, 2, 0, 1),
    (SUM, 3, 1, 1), (FINISH, 7), (SUM, 3, 0, 0), (FINISH, 6), (FINISH, 5), (SUM, 3, 0, 1),
    (FINISH, 4), (FINISH, 2), (FINISH, 3), (FINISH, 1), (FINISH, 0),
)
PLACE = (0, 1, 2, 5, 6, 7, 3, 4)
NEARER = 5
SPARE = (tuple(range(14)), tuple(range(12)) + (14, 15))
VMEM_LIMIT = 32 * 1024 * 1024


def iota(shape, axis):
    return lax.broadcasted_iota(jnp.int32, shape, axis)


def routing(y, ids_ref, gw_ref, pick_ref, place_ref, pad):
    tok = ids_ref.shape[1]
    pad[...] = jnp.zeros_like(pad)
    pad[0:2, 0:tok] = ids_ref[...].astype(F32)
    pad[2:4, 0:tok] = pick_ref[...].astype(F32)
    pad[4:6, 0:tok] = gw_ref[...]
    pad[8:9, 0:N] = place_ref[...].astype(F32)
    wide = pad[0:8, :]
    wide = (
        wide
        + pltpu.roll(wide, tok, 1)
        + pltpu.roll(wide, 2 * tok, 1)
        + pltpu.roll(wide, 3 * tok, 1)
    )
    place_row = jnp.broadcast_to(pad[8:9, :], (N, 128))
    sub, lane = iota((N, 128), 0), iota((N, 128), 1)
    place_col = jnp.sum(jnp.where(sub == lane, place_row, 0.0), axis=1, keepdims=True)
    before = jnp.sum(
        jnp.where((place_row == place_col) & (lane < sub), 1.0, 0.0), axis=1, keepdims=True
    )
    subf = sub.astype(F32)
    row, col = iota((128, 128), 0), iota((128, 128), 1)
    j = row // ROWS
    offs = jnp.where(j % 2 == 1, (j + 1) // 2, -(j // 2))
    copy_of_row = ((y - offs + N) % N).astype(F32)
    chosen = []
    for k in range(2):
        match = place_col == wide[k : k + 1, :]
        copies = jnp.sum(jnp.where(match, 1.0, 0.0), axis=0, keepdims=True)
        wanted = jnp.where(copies > 1.5, wide[2 + k : 3 + k, :], 0.0)
        phys = jnp.sum(
            jnp.where(match & (before == wanted), subf, 0.0), axis=0, keepdims=True
        )
        chosen.append(jnp.where(copy_of_row == phys, 1.0, 0.0))
    earlier = jnp.where((row // tok == col // tok) & (row < col), 1.0, 0.0).astype(BF16)
    rank = jnp.dot((chosen[0] + chosen[1]).astype(BF16), earlier, preferred_element_type=F32)
    own = col // tok == (row // CAP) % FOLD
    slot = (row % CAP).astype(F32)
    in0 = jnp.where(own & (rank == slot), chosen[0], 0.0)
    in1 = jnp.where(own & (rank + chosen[0] == slot), chosen[1], 0.0)
    pick = (in0 + in1).astype(BF16)
    combine = in0 * wide[4:5, :] + in1 * wide[5:6, :]
    return pick, combine.T


def kernel(
    ids_hbm, gw_hbm, pick_hbm, place_hbm, tok_hbm, win_ref, wout_ref, out_ref,
    ids_ref, gw_ref, pick_ref, place_ref, tok_ref,
    pad, w1, w2, comb, ybuf, xbuf, xrows, part, sbuf, rbuf, obuf, cbuf, res,
    lsem, sent, ydr, agr, agl, rsr, yrr,
):
    wide = tok_ref.shape[1] // FOLD
    units = wout_ref.shape[0]
    e = lax.axis_index("expert")
    y, z = e // N, e % N
    right = y * N + (z + 1) % N
    left = y * N + (z + N - 1) % N
    side = (right, left)

    barrier = pltpu.get_barrier_semaphore()
    peers = [(y + d) % N * N + z for d in (4, 3, 5, 2, 6, 1, 7)] + [right, left]
    for peer in peers:
        pl.semaphore_signal(barrier, inc=1, device_id={"expert": peer}, device_id_type=MESH)

    pairs = (
        (ids_hbm, ids_ref), (gw_hbm, gw_ref), (pick_hbm, pick_ref), (place_hbm, place_ref),
        (tok_hbm, tok_ref), (win_ref.at[0], w1.at[:, 0:units]),
        (win_ref.at[1], w1.at[:, units : 2 * units]),
    ) + tuple(
        (wout_ref.at[:, q * wide : (q + 1) * wide], w2.at[q // 2, q % 2 * units : (q % 2 + 1) * units])
        for q in range(FOLD)
    )
    loads = [pltpu.make_async_copy(src, dst, lsem.at[n]) for n, (src, dst) in enumerate(pairs)]
    for load in loads:
        load.start()
    for load in loads[:5]:
        load.wait()

    pick, combine = routing(y, ids_ref, gw_ref, pick_ref, place_ref, pad)
    tok_fold = jnp.concatenate(
        [tok_ref[:, q * wide : (q + 1) * wide] for q in range(FOLD)], axis=0
    )
    messages = jnp.dot(
        pick[:, : tok_fold.shape[0]], tok_fold, preferred_element_type=F32
    ).astype(BF16)
    ybuf[...] = messages
    xbuf[0, 0, 0:ROWS, :] = messages[0:ROWS]
    half_rows = combine[: tok_fold.shape[0]]
    high = half_rows.astype(BF16)
    comb[...] = jnp.concatenate([high, (half_rows - high.astype(F32)).astype(BF16)], axis=0)

    pl.semaphore_wait(barrier, len(peers))

    def remote(src, dst, send, recv, target):
        return pltpu.make_async_remote_copy(
            src_ref=src, dst_ref=dst, send_sem=send, recv_sem=recv,
            device_id={"expert": target}, device_id_type=MESH,
        )

    def msg(i, count=1):
        return slice(i * ROWS, (i + count) * ROWS)

    y_in = {}
    for j in range(1, N):
        y_in[j] = remote(
            ybuf.at[msg(j)], xbuf.at[j // 4, 0, msg(j % 4)], sent.at[0], ydr.at[j],
            (y - OFFS[j] + N) % N * N + z,
        )
        y_in[j].start()

    def hop(s, m, d):
        h, i = m // 4, m % 4
        src = (N - s) % N if d == 0 else s
        dst = N - 1 - s if d == 0 else s + 1
        if s < 2:
            arrival = agr.at[d, 8 * s + m]
        elif s == 2 and i in FAR[d]:
            arrival = agr.at[d, 16 + 2 * h + i % 2]
        else:
            arrival = agl.at[h, d, s - 2]
        return remote(
            xbuf.at[h, src, msg(i)], xbuf.at[h, dst, msg(i)], sent.at[1], arrival, side[d]
        )

    waited = {}

    def relay(s, m, d):
        if s > 0:
            hop(s - 1, m, d).wait_recv()
        elif d == 0 and m > 0:
            y_in[m].wait_recv()
        hop(s, m, d).start()
        if s > 0 or d == 0:
            key = m // 4, (N - s) % N if d == 0 else s
            waited[key] = waited.get(key, 0) + 1
            if waited[key] == 4:
                unfold(*key)

    def arrived(h):
        for d in range(2):
            for slot, first in ((5 - 2 * d, FAR[1 - d][0]), (4, FAR[d][0])):
                rows = xbuf.at[h, slot, msg(first, 2)]
                remote(
                    rows, rows, sent.at[1], agl.at[h, d, 1 if slot == 4 else 0], side[d]
                ).wait_recv()
        for slot in (5, 3, 4):
            unfold(h, slot)

    a, b = iota((4 * ROWS, 4 * ROWS), 0), iota((4 * ROWS, 4 * ROWS), 1)
    swap = jnp.where(
        (a // 16 == (b // 4) % 4) & ((a // 4) % 4 == b // 16) & (a % 4 == b % 4), 1.0, 0.0
    ).astype(BF16)

    def unfold(h, slot):
        rows = jnp.dot(swap, xbuf[h, slot], preferred_element_type=F32).astype(BF16)
        for q in range(FOLD):
            xrows[h, msg(PLACE[slot]), q * wide : (q + 1) * wide] = rows[msg(q)]

    def expert(h, low, high):
        gate_up = jnp.dot(xrows[h, low:high], w1[...], preferred_element_type=F32)
        gate = gate_up[:, :units]
        act = (gate / (1.0 + jnp.exp(-gate)) * gate_up[:, units:]).astype(BF16)
        rows = high - low
        r, c = iota((2 * rows, rows), 0), iota((2 * rows, rows), 1)
        twice = jnp.where((r // 8 == c // 4) & (r % 4 == c % 4), 1.0, 0.0).astype(BF16)
        spread = jnp.dot(twice, act, preferred_element_type=F32)
        odd = iota(spread.shape, 0) // 4 % 2 == 1
        hidden = jnp.concatenate(
            [jnp.where(odd, 0.0, spread), jnp.where(odd, spread, 0.0)], axis=1
        ).astype(BF16)
        for pair in range(2):
            part[h, pair, 2 * low : 2 * high] = jnp.dot(
                hidden, w2[pair], preferred_element_type=F32
            )

    loaded = []

    def early(h):
        if not loaded:
            for load in loads[5:]:
                load.wait()
            loaded.append(h)
        expert(h, 0, NEARER * ROWS)

    def late(h):
        expert(h, NEARER * ROWS, N * ROWS)

    def partial_sum(m, slot):
        first = 32 * PLACE[slot] + 8 * (m % 4)
        rows = slice(first, first + 8)
        return jnp.concatenate([part[m // 4, 0, rows, :], part[m // 4, 1, rows, :]], axis=0)

    def ring(d, s, m):
        if m % 4 in FAR[d]:
            at = 4 * s + 2 * (m // 4) + m % 2
        else:
            at = 12 + 4 * s + 2 * (m // 4) + m % 2
        spare = len(SPARE[d])
        arrival = agr.at[d, SPARE[d][at]] if at < spare else rsr.at[d, at - spare]
        copy = remote(sbuf.at[d, at], rbuf.at[d, at], sent.at[2], arrival, side[d])
        return copy, at

    def add_on(s, m, d):
        value = partial_sum(m, 4 - s if d == 0 else 4 + s)
        if s > (0 if m % 4 in FAR[d] else 1):
            earlier, at = ring(d, s - 1, m)
            earlier.wait_recv()
            value = value + rbuf[d, at].astype(F32)
        copy, at = ring(d, s, m)
        sbuf[d, at] = value.astype(BF16)
        copy.start()

    def finish(m):
        value = partial_sum(m, 0)
        for d in range(2):
            last, at = ring(d, 3, m)
            last.wait_recv()
            value = value + rbuf[d, at].astype(F32)
        if m == 0:
            cbuf[0:ROWS, :] = value.astype(BF16)
            return
        obuf[msg(m)] = value.astype(BF16)
        remote(
            obuf.at[msg(m)], cbuf.at[msg(m)], sent.at[3], yrr.at[0],
            (y + OFFS[m] + N) % N * N + z,
        ).start()

    steps = {
        RELAY: relay, ARRIVED: arrived, EARLY: early, LATE: late, SUM: add_on, FINISH: finish
    }
    for kind, *which in PROGRAM:
        steps[kind](*which)
    others = cbuf.at[ROWS : N * ROWS]
    remote(others, others, sent.at[3], yrr.at[0], right).wait_recv()
    both = jnp.dot(comb[...], cbuf[...], preferred_element_type=F32)
    half = both.shape[0] // 2
    result = both[:half] + both[half:]
    tok = tok_ref.shape[0]
    for q in range(FOLD):
        res[:, q * wide : (q + 1) * wide] = result[q * tok : (q + 1) * tok].astype(BF16)
    store = pltpu.make_async_copy(res, out_ref, lsem.at[0])
    store.start()
    for sem, whole in (
        (0, ybuf.at[ROWS : N * ROWS]), (1, xbuf.at[:, 0:7]), (2, sbuf), (3, obuf.at[ROWS : N * ROWS])
    ):
        remote(whole, whole, sent.at[sem], yrr.at[0], right).wait_send()
    store.wait()


def body(tokens, expert_ids, gate_weights, replica_pick, placement, w_in, w_out):
    tok, width = tokens.shape
    units = w_out.shape[0]
    wide = width // FOLD
    dma = pltpu.SemaphoreType.DMA
    operands = (
        expert_ids.T, gate_weights.T, replica_pick.T, placement.reshape(1, -1), tokens,
        w_in, w_out,
    )
    return pl.pallas_call(
        kernel,
        out_shape=jax.ShapeDtypeStruct((tok, width), BF16),
        in_specs=[pl.BlockSpec(memory_space=pl.ANY)] * 7,
        out_specs=pl.BlockSpec(memory_space=pl.ANY),
        scratch_shapes=[pltpu.VMEM(x.shape, x.dtype) for x in operands[:5]]
        + [
            pltpu.VMEM((16, 128), F32),
            pltpu.VMEM((width, 2 * units), BF16),
            pltpu.VMEM((2, 2 * units, wide), BF16),
            pltpu.VMEM((2 * FOLD * tok, 128), BF16),
            pltpu.VMEM((N * ROWS, wide), BF16),
            pltpu.VMEM((2, N, 4 * ROWS, wide), BF16),
            pltpu.VMEM((2, N * ROWS, width), BF16),
            pltpu.VMEM((2, 2, 2 * N * ROWS, wide), F32),
            pltpu.VMEM((2, 28, ROWS, wide), BF16),
            pltpu.VMEM((2, 28, ROWS, wide), BF16),
            pltpu.VMEM((N * ROWS, wide), BF16),
            pltpu.VMEM((N * ROWS, wide), BF16),
            pltpu.VMEM((tok, width), BF16),
            dma((11,)),
            dma((4,)),
            dma((N,)),
            dma((2, 20)),
            dma((2, 2, 2)),
            dma((2, 14)),
            dma((1,)),
        ],
        compiler_params=pltpu.CompilerParams(
            collective_id=0, has_side_effects=True, vmem_limit_bytes=VMEM_LIMIT
        ),
    )(*[pltpu.with_memory_space_constraint(x, pltpu.HBM) for x in operands])


def solution(mesh):
    in_specs = (
        P(("dp", "expert"), None),
        P(("dp", "expert"), None),
        P(("dp", "expert"), None),
        P(("dp", "expert"), None),
        P(),
        P(None, None, "expert"),
        P("expert", None),
    )
    out_specs = P(("dp", "expert"), None)
    return jax.shard_map(body, mesh=mesh, in_specs=in_specs, out_specs=out_specs, check_vma=False)
```

```python
import jax
import jax.numpy as jnp
from jax import lax
from jax.experimental import pallas as pl
from jax.experimental.pallas import tpu as pltpu
from jax.sharding import PartitionSpec as P

N = 8
OFFS = (0, 1, -1, 2, -2, 3, -3, 4)
FOLD = 4
CAP = 4
ROWS = FOLD * CAP
MESH = pl.DeviceIdType.MESH
F32 = jnp.float32
BF16 = jnp.bfloat16
FAR = ((0, 1), (2, 3))
RELAY, ARRIVED, EARLY, LATE, SUM, FINISH = range(6)
PROGRAM = (
    (RELAY, 0, 0, 0), (RELAY, 0, 0, 1), (RELAY, 0, 1, 0), (RELAY, 0, 1, 1), (RELAY, 0, 2, 0),
    (RELAY, 0, 2, 1), (RELAY, 1, 0, 1), (RELAY, 1, 0, 0), (RELAY, 0, 3, 0), (RELAY, 0, 3, 1),
    (RELAY, 0, 4, 0), (RELAY, 0, 4, 1), (RELAY, 0, 5, 0), (RELAY, 0, 5, 1), (RELAY, 1, 1, 0),
    (RELAY, 1, 1, 1), (RELAY, 0, 7, 0), (RELAY, 0, 7, 1), (RELAY, 1, 2, 0), (RELAY, 0, 6, 0),
    (RELAY, 0, 6, 1), (RELAY, 1, 2, 1), (RELAY, 1, 4, 0), (RELAY, 1, 3, 1), (RELAY, 2, 0, 0),
    (RELAY, 1, 5, 0), (RELAY, 1, 4, 1), (RELAY, 2, 0, 1), (RELAY, 1, 7, 1), (RELAY, 1, 3, 0),
    (RELAY, 2, 1, 0), (RELAY, 1, 7, 0), (RELAY, 1, 6, 1), (RELAY, 2, 2, 1), (RELAY, 2, 3, 1),
    (RELAY, 2, 4, 0), (RELAY, 1, 5, 1), (RELAY, 1, 6, 0), (RELAY, 2, 2, 0), (RELAY, 2, 5, 0),
    (RELAY, 2, 1, 1), (RELAY, 2, 7, 1), (RELAY, 2, 6, 1), (RELAY, 3, 0, 0), (RELAY, 2, 3, 0),
    (RELAY, 3, 2, 1), (RELAY, 3, 3, 1), (RELAY, 3, 1, 0), (RELAY, 2, 5, 1), (RELAY, 2, 6, 0),
    (RELAY, 3, 4, 0), (RELAY, 2, 7, 0), (RELAY, 2, 4, 1), (RELAY, 3, 7, 1), (RELAY, 3, 5, 0),
    (RELAY, 3, 6, 1), (EARLY, 0), (ARRIVED, 0), (LATE, 0), (SUM, 0, 2, 1), (SUM, 0, 1, 0),
    (SUM, 1, 3, 0), (SUM, 1, 1, 1), (SUM, 1, 0, 1), (SUM, 0, 0, 0), (SUM, 1, 2, 0), (SUM, 0, 3, 1),
    (EARLY, 1), (ARRIVED, 1), (LATE, 1), (SUM, 0, 7, 1), (SUM, 0, 4, 0), (SUM, 0, 5, 0),
    (SUM, 0, 6, 1), (SUM, 1, 7, 0), (SUM, 1, 2, 1), (SUM, 1, 6, 0), (SUM, 1, 1, 0), (SUM, 2, 1, 1),
    (SUM, 2, 3, 0), (SUM, 1, 4, 1), (SUM, 1, 5, 1), (SUM, 1, 7, 1), (SUM, 1, 4, 0), (SUM, 1, 3, 1),
    (SUM, 1, 5, 0), (SUM, 2, 2, 0), (SUM, 1, 6, 1), (SUM, 2, 2, 1), (SUM, 1, 0, 0), (SUM, 2, 7, 0),
    (SUM, 2, 1, 0), (SUM, 2, 4, 1), (SUM, 2, 6, 0), (SUM, 3, 3, 0), (SUM, 2, 5, 1), (SUM, 2, 7, 1),
    (SUM, 2, 3, 1), (SUM, 2, 6, 1), (SUM, 2, 5, 0), (SUM, 3, 2, 1), (SUM, 2, 4, 0), (SUM, 2, 0, 0),
    (SUM, 3, 4, 1), (SUM, 3, 5, 1), (SUM, 3, 7, 0), (SUM, 3, 7, 1), (SUM, 3, 6, 0), (SUM, 3, 2, 0),
    (SUM, 3, 3, 1), (SUM, 3, 6, 1), (SUM, 2, 0, 1), (SUM, 3, 5, 0), (SUM, 3, 4, 0), (SUM, 3, 1, 0),
    (SUM, 3, 1, 1), (SUM, 3, 0, 0), (FINISH, 7), (FINISH, 6), (SUM, 3, 0, 1), (FINISH, 5),
    (FINISH, 4), (FINISH, 2), (FINISH, 3), (FINISH, 1), (FINISH, 0),
)
PLACE = (0, 1, 2, 5, 6, 7, 3, 4)
NEARER = 5
SPARE = (tuple(range(14)), tuple(range(12)) + (14, 15))
VMEM_LIMIT = 32 * 1024 * 1024


def iota(shape, axis):
    return lax.broadcasted_iota(jnp.int32, shape, axis)


def routing(y, ids_ref, gw_ref, pick_ref, place_ref, pad):
    tok = ids_ref.shape[1]
    pad[...] = jnp.zeros_like(pad)
    pad[0:2, 0:tok] = ids_ref[...].astype(F32)
    pad[2:4, 0:tok] = pick_ref[...].astype(F32)
    pad[4:6, 0:tok] = gw_ref[...]
    pad[8:9, 0:N] = place_ref[...].astype(F32)
    wide = pad[0:8, :]
    wide = (
        wide
        + pltpu.roll(wide, tok, 1)
        + pltpu.roll(wide, 2 * tok, 1)
        + pltpu.roll(wide, 3 * tok, 1)
    )
    place_row = jnp.broadcast_to(pad[8:9, :], (N, 128))
    sub, lane = iota((N, 128), 0), iota((N, 128), 1)
    place_col = jnp.sum(jnp.where(sub == lane, place_row, 0.0), axis=1, keepdims=True)
    before = jnp.sum(
        jnp.where((place_row == place_col) & (lane < sub), 1.0, 0.0), axis=1, keepdims=True
    )
    subf = sub.astype(F32)
    row, col = iota((128, 128), 0), iota((128, 128), 1)
    j = row // ROWS
    offs = jnp.where(j % 2 == 1, (j + 1) // 2, -(j // 2))
    copy_of_row = ((y - offs + N) % N).astype(F32)
    chosen = []
    for k in range(2):
        match = place_col == wide[k : k + 1, :]
        copies = jnp.sum(jnp.where(match, 1.0, 0.0), axis=0, keepdims=True)
        wanted = jnp.where(copies > 1.5, wide[2 + k : 3 + k, :], 0.0)
        phys = jnp.sum(
            jnp.where(match & (before == wanted), subf, 0.0), axis=0, keepdims=True
        )
        chosen.append(jnp.where(copy_of_row == phys, 1.0, 0.0))
    earlier = jnp.where((row // tok == col // tok) & (row < col), 1.0, 0.0).astype(BF16)
    rank = jnp.dot((chosen[0] + chosen[1]).astype(BF16), earlier, preferred_element_type=F32)
    own = col // tok == (row // CAP) % FOLD
    slot = (row % CAP).astype(F32)
    in0 = jnp.where(own & (rank == slot), chosen[0], 0.0)
    in1 = jnp.where(own & (rank + chosen[0] == slot), chosen[1], 0.0)
    pick = (in0 + in1).astype(BF16)
    combine = in0 * wide[4:5, :] + in1 * wide[5:6, :]
    return pick, combine.T


def kernel(
    ids_hbm, gw_hbm, pick_hbm, place_hbm, tok_hbm, win_ref, wout_ref, out_ref,
    ids_ref, gw_ref, pick_ref, place_ref, tok_ref,
    pad, w1, w2, comb, ybuf, xbuf, xrows, part, sbuf, rbuf, obuf, cbuf, res,
    lsem, sent, ydr, agr, agl, rsr, yrr,
):
    wide = tok_ref.shape[1] // FOLD
    units = wout_ref.shape[0]
    e = lax.axis_index("expert")
    y, z = e // N, e % N
    right = y * N + (z + 1) % N
    left = y * N + (z + N - 1) % N
    side = (right, left)

    barrier = pltpu.get_barrier_semaphore()
    peers = [(y + d) % N * N + z for d in (4, 3, 5, 2, 6, 1, 7)] + [right, left]
    for peer in peers:
        pl.semaphore_signal(barrier, inc=1, device_id={"expert": peer}, device_id_type=MESH)

    pairs = (
        (ids_hbm, ids_ref), (gw_hbm, gw_ref), (pick_hbm, pick_ref), (place_hbm, place_ref),
        (tok_hbm, tok_ref), (win_ref.at[0], w1.at[:, 0:units]),
        (win_ref.at[1], w1.at[:, units : 2 * units]),
    ) + tuple(
        (wout_ref.at[:, q * wide : (q + 1) * wide], w2.at[q // 2, q % 2 * units : (q % 2 + 1) * units])
        for q in range(FOLD)
    )
    loads = [pltpu.make_async_copy(src, dst, lsem.at[n]) for n, (src, dst) in enumerate(pairs)]
    for load in loads:
        load.start()
    for load in loads[:5]:
        load.wait()

    pick, combine = routing(y, ids_ref, gw_ref, pick_ref, place_ref, pad)
    tok_fold = jnp.concatenate(
        [tok_ref[:, q * wide : (q + 1) * wide] for q in range(FOLD)], axis=0
    )
    messages = jnp.dot(
        pick[:, : tok_fold.shape[0]], tok_fold, preferred_element_type=F32
    ).astype(BF16)
    ybuf[...] = messages
    xbuf[0, 0, 0:ROWS, :] = messages[0:ROWS]
    half_rows = combine[: tok_fold.shape[0]]
    high = half_rows.astype(BF16)
    comb[...] = jnp.concatenate([high, (half_rows - high.astype(F32)).astype(BF16)], axis=0)

    pl.semaphore_wait(barrier, len(peers))

    def remote(src, dst, send, recv, target):
        return pltpu.make_async_remote_copy(
            src_ref=src, dst_ref=dst, send_sem=send, recv_sem=recv,
            device_id={"expert": target}, device_id_type=MESH,
        )

    def msg(i, count=1):
        return slice(i * ROWS, (i + count) * ROWS)

    y_in = {}
    for j in range(1, N):
        y_in[j] = remote(
            ybuf.at[msg(j)], xbuf.at[j // 4, 0, msg(j % 4)], sent.at[0], ydr.at[j],
            (y - OFFS[j] + N) % N * N + z,
        )
        y_in[j].start()

    def hop(s, m, d):
        h, i = m // 4, m % 4
        src = (N - s) % N if d == 0 else s
        dst = N - 1 - s if d == 0 else s + 1
        if s < 2:
            arrival = agr.at[d, 8 * s + m]
        elif s == 2 and i in FAR[d]:
            arrival = agr.at[d, 16 + 2 * h + i % 2]
        else:
            arrival = agl.at[h, d, s - 2]
        return remote(
            xbuf.at[h, src, msg(i)], xbuf.at[h, dst, msg(i)], sent.at[1], arrival, side[d]
        )

    waited = {}

    def relay(s, m, d):
        if s > 0:
            hop(s - 1, m, d).wait_recv()
        elif d == 0 and m > 0:
            y_in[m].wait_recv()
        hop(s, m, d).start()
        if s > 0 or d == 0:
            key = m // 4, (N - s) % N if d == 0 else s
            waited[key] = waited.get(key, 0) + 1
            if waited[key] == 4:
                unfold(*key)

    def arrived(h):
        for d in range(2):
            for slot, first in ((5 - 2 * d, FAR[1 - d][0]), (4, FAR[d][0])):
                rows = xbuf.at[h, slot, msg(first, 2)]
                remote(
                    rows, rows, sent.at[1], agl.at[h, d, 1 if slot == 4 else 0], side[d]
                ).wait_recv()
        for slot in (5, 3, 4):
            unfold(h, slot)

    a, b = iota((4 * ROWS, 4 * ROWS), 0), iota((4 * ROWS, 4 * ROWS), 1)
    swap = jnp.where(
        (a // 16 == (b // 4) % 4) & ((a // 4) % 4 == b // 16) & (a % 4 == b % 4), 1.0, 0.0
    ).astype(BF16)

    def unfold(h, slot):
        rows = jnp.dot(swap, xbuf[h, slot], preferred_element_type=F32).astype(BF16)
        for q in range(FOLD):
            xrows[h, msg(PLACE[slot]), q * wide : (q + 1) * wide] = rows[msg(q)]

    def expert(h, low, high):
        gate_up = jnp.dot(xrows[h, low:high], w1[...], preferred_element_type=F32)
        gate = gate_up[:, :units]
        act = (gate / (1.0 + jnp.exp(-gate)) * gate_up[:, units:]).astype(BF16)
        rows = high - low
        r, c = iota((2 * rows, rows), 0), iota((2 * rows, rows), 1)
        twice = jnp.where((r // 8 == c // 4) & (r % 4 == c % 4), 1.0, 0.0).astype(BF16)
        spread = jnp.dot(twice, act, preferred_element_type=F32)
        odd = iota(spread.shape, 0) // 4 % 2 == 1
        hidden = jnp.concatenate(
            [jnp.where(odd, 0.0, spread), jnp.where(odd, spread, 0.0)], axis=1
        ).astype(BF16)
        for pair in range(2):
            part[h, pair, 2 * low : 2 * high] = jnp.dot(
                hidden, w2[pair], preferred_element_type=F32
            )

    loaded = []

    def early(h):
        if not loaded:
            for load in loads[5:]:
                load.wait()
            loaded.append(h)
        expert(h, 0, NEARER * ROWS)

    def late(h):
        expert(h, NEARER * ROWS, N * ROWS)

    def partial_sum(m, slot):
        first = 32 * PLACE[slot] + 8 * (m % 4)
        rows = slice(first, first + 8)
        return jnp.concatenate([part[m // 4, 0, rows, :], part[m // 4, 1, rows, :]], axis=0)

    def ring(d, s, m):
        if m % 4 in FAR[d]:
            at = 4 * s + 2 * (m // 4) + m % 2
        else:
            at = 12 + 4 * s + 2 * (m // 4) + m % 2
        spare = len(SPARE[d])
        arrival = agr.at[d, SPARE[d][at]] if at < spare else rsr.at[d, at - spare]
        copy = remote(sbuf.at[d, at], rbuf.at[d, at], sent.at[2], arrival, side[d])
        return copy, at

    def add_on(s, m, d):
        value = partial_sum(m, 4 - s if d == 0 else 4 + s)
        if s > (0 if m % 4 in FAR[d] else 1):
            earlier, at = ring(d, s - 1, m)
            earlier.wait_recv()
            value = value + rbuf[d, at].astype(F32)
        copy, at = ring(d, s, m)
        sbuf[d, at] = value.astype(BF16)
        copy.start()

    def finish(m):
        value = partial_sum(m, 0)
        for d in range(2):
            last, at = ring(d, 3, m)
            last.wait_recv()
            value = value + rbuf[d, at].astype(F32)
        if m == 0:
            cbuf[0:ROWS, :] = value.astype(BF16)
            return
        obuf[msg(m)] = value.astype(BF16)
        remote(
            obuf.at[msg(m)], cbuf.at[msg(m)], sent.at[3], yrr.at[0],
            (y + OFFS[m] + N) % N * N + z,
        ).start()

    steps = {
        RELAY: relay, ARRIVED: arrived, EARLY: early, LATE: late, SUM: add_on, FINISH: finish
    }
    for kind, *which in PROGRAM:
        steps[kind](*which)
    others = cbuf.at[ROWS : N * ROWS]
    remote(others, others, sent.at[3], yrr.at[0], right).wait_recv()
    both = jnp.dot(comb[...], cbuf[...], preferred_element_type=F32)
    half = both.shape[0] // 2
    result = both[:half] + both[half:]
    tok = tok_ref.shape[0]
    for q in range(FOLD):
        res[:, q * wide : (q + 1) * wide] = result[q * tok : (q + 1) * tok].astype(BF16)
    store = pltpu.make_async_copy(res, out_ref, lsem.at[0])
    store.start()
    for sem, whole in (
        (0, ybuf.at[ROWS : N * ROWS]), (1, xbuf.at[:, 0:7]), (2, sbuf), (3, obuf.at[ROWS : N * ROWS])
    ):
        remote(whole, whole, sent.at[sem], yrr.at[0], right).wait_send()
    store.wait()


def body(tokens, expert_ids, gate_weights, replica_pick, placement, w_in, w_out):
    tok, width = tokens.shape
    units = w_out.shape[0]
    wide = width // FOLD
    dma = pltpu.SemaphoreType.DMA
    operands = (
        expert_ids.T, gate_weights.T, replica_pick.T, placement.reshape(1, -1), tokens,
        w_in, w_out,
    )
    return pl.pallas_call(
        kernel,
        out_shape=jax.ShapeDtypeStruct((tok, width), BF16),
        in_specs=[pl.BlockSpec(memory_space=pl.ANY)] * 7,
        out_specs=pl.BlockSpec(memory_space=pl.ANY),
        scratch_shapes=[pltpu.VMEM(x.shape, x.dtype) for x in operands[:5]]
        + [
            pltpu.VMEM((16, 128), F32),
            pltpu.VMEM((width, 2 * units), BF16),
            pltpu.VMEM((2, 2 * units, wide), BF16),
            pltpu.VMEM((2 * FOLD * tok, 128), BF16),
            pltpu.VMEM((N * ROWS, wide), BF16),
            pltpu.VMEM((2, N, 4 * ROWS, wide), BF16),
            pltpu.VMEM((2, N * ROWS, width), BF16),
            pltpu.VMEM((2, 2, 2 * N * ROWS, wide), F32),
            pltpu.VMEM((2, 28, ROWS, wide), BF16),
            pltpu.VMEM((2, 28, ROWS, wide), BF16),
            pltpu.VMEM((N * ROWS, wide), BF16),
            pltpu.VMEM((N * ROWS, wide), BF16),
            pltpu.VMEM((tok, width), BF16),
            dma((11,)),
            dma((4,)),
            dma((N,)),
            dma((2, 20)),
            dma((2, 2, 2)),
            dma((2, 14)),
            dma((1,)),
        ],
        compiler_params=pltpu.CompilerParams(
            collective_id=0, has_side_effects=True, vmem_limit_bytes=VMEM_LIMIT
        ),
    )(*[pltpu.with_memory_space_constraint(x, pltpu.HBM) for x in operands])


def solution(mesh):
    in_specs = (
        P(("dp", "expert"), None),
        P(("dp", "expert"), None),
        P(("dp", "expert"), None),
        P(("dp", "expert"), None),
        P(),
        P(None, None, "expert"),
        P("expert", None),
    )
    out_specs = P(("dp", "expert"), None)
    return jax.shard_map(body, mesh=mesh, in_specs=in_specs, out_specs=out_specs, check_vma=False)
```
